128 devices in a mesh: px: 8 (over y, core), py: 16 (over x, z).
Axes of the slice: x: 4, y: 4, z: 4, core: 2. Of those that a mesh axis runs over, the one named last changes fastest.
Arguments:
- control_start: float32 [2, 16, 128, 2048], P(None, 'py', None, 'px'), may hold values from -12 to 12
- coef_x: float32 [16, 128, 2048], P('py', None, 'px'), may hold values from 0.1 to 0.45
- coef_y: float32 [16, 128, 2048], P('py', 'px'), may hold values from 0.1 to 0.45
- innovation: float32 [131072, 128], P(('px', 'py')), may hold values from -6 to 6
- obs_weight: float32 [131072, 128], P(('px', 'py')), may hold values from 0.25 to 4
- interp: float32 [131072], P(('px', 'py')), may hold values from 0 to 1
- obs_owner: int32 [131072, 1], P(('px', 'py')), may hold values from 0 to 15; in each aligned block of 1024 rows (0 to 1023, 1024 to 2047, ...) at most 192 rows name the same one
- cell_key: int32 [131072], P(('px', 'py')), may hold values from 0 to 31
- stencil: int32 [131072], P(('px', 'py')), may hold values from 0 to 14
Outputs:
- control: float32 [2, 16, 128, 2048], P(None, 'py', None, 'px')
- residual: float32 [2, 16, 128, 2048], P(None, 'py', None, 'px')
The draws below stay inside these ranges and needn't reach their ends.
Inputs may be any that keep to these rules, and one draw needn't show every extreme that they name: `obs_owner`: at most 192 of the observation rows of one device name the same owner, and exactly 192 do for some owner on some device.
All inputs are finite; a program needn't handle non-finite values.
Results may differ from the reference program's by a relative error of at most 0.00023.
Values sent between devices are 32-bit elements; how exact they have to be, the bound alone decides.
A program may use at most 64 MiB of HBM per device.

```python
import math
import jax
import jax.numpy as jnp
import numpy as np
from jax import lax

F = 2
SEG = 128
M = 4
ITERS = 2
LZ = 1
LX = 16
NY = 2048
OBS_DEV = 1024
NX = 128
NZ = 16
NB = 16
CAP = 192
PX_ROWS = 16384
OBS = 131072
N_PY = 16


def draw_control_start(key, part):
    y_frac = jnp.arange(NY, dtype=jnp.float32) / NY
    z_frac = jnp.arange(NZ, dtype=jnp.float32) / NZ
    random_part = jnp.clip(jax.random.normal(key, (F, NZ, NX, NY), jnp.float32), -4.0, 4.0)
    row_scale = (0.5 + y_frac)[None, None, None, :] * (1.0 + z_frac)[None, :, None, None]
    return random_part * row_scale


def set_ends(values, stream_key, smallest, high):
    index_at = [jax.random.randint(jax.random.fold_in(stream_key, axis), (), 0, length) for axis, length in enumerate(values.shape)]
    main_axis = values.shape.index(max(values.shape))
    beside = index_at[:main_axis] + [(index_at[main_axis] + 1) % values.shape[main_axis]] + index_at[main_axis + 1:]
    return values.at[tuple(index_at)].set(smallest).at[tuple(beside)].set(high)


def level_of(stream_key, dims, pieces, low, high):
    def one(position, blocks):
        draws = jax.random.uniform(jax.random.fold_in(jax.random.fold_in(stream_key, 6), position), (blocks,), jnp.float32, low / len(pieces), high / len(pieces))
        return jnp.repeat(jnp.exp(draws), dims[position] // blocks).reshape((-1,) + (1,) * (len(dims) - position - 1))

    factor_of = one(*pieces[0])
    for cut in pieces[1:]:
        factor_of = factor_of * one(*cut)
    return factor_of


def deal_out(own_key, own, number, rows, count, top, most, skew):
    sequence = jax.random.permutation(own_key, count)
    heavy_load, ordinary = load_shares(count, rows * top, most, skew, True), load_shares(count, rows * top, most, skew, False)
    places = jnp.arange(count)

    def named(tallies, rotation):
        used = int((tallies > 0).sum())
        fixed = max(1, used // 4)
        passed = fixed + (places - fixed + rotation * (used - fixed)) % max(1, count - fixed)
        return jnp.zeros((count,), jnp.int32).at[sequence[jnp.where(places < fixed, places, passed)]].set(jnp.asarray(tallies, jnp.int32))

    tallies = jnp.where(number % 4 == 0, named(heavy_load, number // 4), named(ordinary, number - number // 4 - 1))
    mixed = jax.random.permutation(jax.random.fold_in(own, 3), count)
    source_of, taker = mixed[0:count // 2 * 2:2], mixed[1:count // 2 * 2:2]
    margin = jnp.minimum(tallies[source_of] - 1, most - tallies[taker]) // 2
    margin = jnp.where((source_of == sequence[0]) | (taker == sequence[0]) | (tallies[taker] == 0), 0, jnp.maximum(margin, 0))
    passed = jax.random.randint(jax.random.fold_in(own, 4), (count // 2,), 0, 1 << 20) % (margin + 1)
    tallies = tallies.at[source_of].add(-passed).at[taker].add(passed)
    labels = jnp.searchsorted(jnp.cumsum(tallies), jnp.arange(rows * top), side="right").astype(jnp.int32)
    listing = labels.reshape(top, rows).T
    listing = listing[jax.random.permutation(jax.random.fold_in(own, 1), rows)]
    rotation = jax.random.randint(jax.random.fold_in(own, 2), (rows, 1), 0, top)
    return jnp.take_along_axis(listing, (jnp.arange(top)[None, :] + rotation) % top, axis=1)


def load_shares(count, total, reach, lean, full):
    weights = [(1 << 20) // math.isqrt(rank ** lean) + 1 for rank in range(1, count + 1)]
    largest = reach if full else min(reach, max(-(-total // count), total * weights[0] // sum(weights)))
    least = 1 if total - largest >= count - 1 else 0
    counts, rest = [largest] + [least] * (count - 1), total - largest - least * (count - 1)
    while rest > 0:
        free = [i for i in range(1, count) if counts[i] < largest] or [i for i in range(1, count) if counts[i] < reach]
        pool, budget = sum([weights[i] for i in free]), rest
        for i in free:
            more = min(reach - counts[i], max(1, budget * weights[i] // pool), rest)
            counts[i] = counts[i] + more
            rest = rest - more
    return np.array(counts)


def normal_values(key, dims, deviation, most, pieces=(), kind=jnp.bfloat16):
    factor_of = level_of(key, dims, pieces, -0.22, 0.18) if pieces else 1.0
    values = jax.random.normal(key, dims, jnp.float32) * deviation * factor_of
    return jnp.minimum(jnp.maximum(values, -most), most).astype(kind)


def setup_inputs(seed: int = 0) -> dict:
    key_list = jax.random.split(jax.random.key(seed), 10)
    control_start = draw_control_start(jax.random.fold_in(key_list[9], 71), 0)
    coef_x = jnp.clip(jnp.exp(math.log(0.45) - 1.50407736 * jax.random.uniform(key_list[1], (NZ, NX, NY), jnp.float32) ** level_of(key_list[1], (NZ, NX, NY), ((0, 16), (2, 8)), -0.2, 0.2)), 0.1, 0.45)
    coef_y = jnp.clip(jnp.exp(math.log(0.45) - 1.50407736 * jax.random.uniform(key_list[2], (NZ, NX, NY), jnp.float32) ** level_of(key_list[2], (NZ, NX, NY), ((0, 16), (1, 8)), -0.2, 0.2)), 0.1, 0.45)
    innovation = normal_values(key_list[3], (OBS, SEG), 1.0, 6.0, ((0, 128),), jnp.float32)
    obs_weight = jnp.clip(jnp.exp(math.log(4.0) - 2.7725887 * jax.random.uniform(key_list[4], (OBS, SEG), jnp.float32) ** level_of(key_list[4], (OBS, SEG), ((0, 128),), -0.2, 0.2)), 0.25, 4.0)
    interp = jnp.clip(1.0 * jax.random.uniform(key_list[5], (OBS,), jnp.float32) ** level_of(key_list[5], (OBS,), ((0, 128),), -0.2, 0.2), 0.0, 1.0)
    obs_owner_keys = jax.random.split(jax.random.fold_in(key_list[6], 1), OBS // OBS_DEV)
    obs_owner_turns = jax.random.permutation(jax.random.fold_in(key_list[6], 3), OBS // OBS_DEV)
    obs_owner = jax.vmap(lambda own, number: deal_out(jax.random.fold_in(key_list[6], 2), own, number, OBS_DEV, N_PY, 1, CAP, 2))(obs_owner_keys, obs_owner_turns).reshape((OBS, 1))
    cell_key = set_ends(jax.random.randint(key_list[7], (OBS,), 0, F * LZ * NB), jax.random.fold_in(key_list[7], 1), 0, (F * LZ * NB) - 1).astype(jnp.int32)
    stencil = set_ends(jax.random.randint(key_list[8], (OBS,), 0, LX - 1), jax.random.fold_in(key_list[8], 1), 0, (LX - 1) - 1).astype(jnp.int32)
    return dict(control_start=control_start, coef_x=coef_x, coef_y=coef_y, innovation=innovation, obs_weight=obs_weight, interp=interp, obs_owner=obs_owner, cell_key=cell_key, stencil=stencil)


def diffuse(values, coeffs, axis_dim):
    length = values.shape[axis_dim]
    face_coef = lax.slice_in_dim(coeffs[None], 0, length - 1, axis=axis_dim)
    pad_after = [(0, 0)] * values.ndim
    pad_before = [(0, 0)] * values.ndim
    pad_after[axis_dim] = (0, 1)
    pad_before[axis_dim] = (1, 0)
    for repeat in range(M):
        next_cell = lax.slice_in_dim(values, 1, length, axis=axis_dim)
        this_cell = lax.slice_in_dim(values, 0, length - 1, axis=axis_dim)
        flux_face = face_coef * (next_cell - this_cell)
        values = values + jnp.pad(flux_face, pad_after) - jnp.pad(flux_face, pad_before)
    return values


def misfit(state_in, observed, weights, shares_in, row_index):
    flat_field = state_in.reshape(-1, SEG)
    lower_rows = flat_field[row_index]
    upper_rows = flat_field[row_index + NB]
    shares = shares_in[:, None]
    modelled = (1.0 - shares) * lower_rows + shares * upper_rows
    weighted = weights * (observed - modelled)
    result = jnp.zeros_like(flat_field).at[row_index].add((1.0 - shares) * weighted)
    result = result.at[row_index + NB].add(shares * weighted)
    return result.reshape(state_in.shape)


def reference(control_start, coef_x, coef_y, innovation, obs_weight, interp, obs_owner, cell_key, stencil):
    coef_x = coef_x.at[:, -1, :].set(0.0)
    coef_y = coef_y.at[:, :, -1].set(0.0)
    rows_all = jnp.arange(OBS, dtype=jnp.int32)
    px_index = rows_all // PX_ROWS
    level_z = obs_owner[:, 0] * LZ + (cell_key // NB) % LZ
    field_id = cell_key // (LZ * NB)
    x_cell = px_index * LX + stencil
    row_index = (((field_id * NZ + level_z) * NX + x_cell) * NB + cell_key % NB).astype(jnp.int32)

    def forward(values_in):
        return diffuse(diffuse(values_in, coef_x, 2), coef_y, 3)

    def adjoint(values_in):
        return diffuse(diffuse(values_in, coef_y, 3), coef_x, 2)

    no_data = jnp.zeros_like(innovation)
    residual = adjoint(misfit(forward(control_start), innovation, obs_weight, interp, row_index)) - control_start
    control = control_start
    direction = residual
    norm_now = jnp.sum(residual * residual)
    for repeat in range(ITERS):
        applied = direction - adjoint(misfit(forward(direction), no_data, obs_weight, interp, row_index))
        step_size = norm_now / jnp.sum(direction * applied)
        control = control + step_size * direction
        residual = residual - step_size * applied
        norm_next = jnp.sum(residual * residual)
        direction = residual + (norm_next / norm_now) * direction
        norm_now = norm_next
    return control, residual
```

```python
import jax
import jax.numpy as jnp
from jax import lax
from jax.experimental import pallas as pl
from jax.experimental.pallas import tpu as pltpu
from jax.sharding import PartitionSpec as P

NPX = 8
NPY = 16
CAP = 192
ROWS = 1024
L = 128
M = 4
NB = 16
T = 512
f32 = jnp.float32
bf16 = jnp.bfloat16
MESH = pl.DeviceIdType.MESH
NT = (((1,), (1,)), ((), ()))
TN = (((0,), (0,)), ((), ()))


def dot(a, b):
    return jnp.dot(a, b, preferred_element_type=f32)


def iota(shape, axis):
    return lax.broadcasted_iota(jnp.int32, shape, axis)


def split(v):
    hi = v.astype(bf16)
    return hi, (v - hi.astype(f32)).astype(bf16)


def xsweep(v, c):
    for _ in range(M):
        flux = c * (pltpu.roll(v, L - 1, 0) - v)
        v = v + flux - pltpu.roll(flux, 1, 0)
    return v


def ysweep(v, c, last, first):
    for _ in range(M):
        r = [pltpu.roll(t, L - 1, 1) for t in v]
        flux = [c[j] * (jnp.where(last, r[(j + 1) % 3], r[j]) - v[j]) for j in range(3)]
        r = [pltpu.roll(t, 1, 1) for t in flux]
        v = [v[j] + flux[j] - jnp.where(first, r[(j + 2) % 3], r[j]) for j in range(3)]
    return v


def tri(u, d, e):
    eu = e * u
    return d * u + e * pltpu.roll(u, u.shape[0] - 1, 0) + pltpu.roll(eu, 1, 0)


def kernel(
    own, key, sten, itp, inn, wgt, cin, cxin, cyin, ctl, res,
    keys, vals, metaq, pbuf, sw, sd, sm, rw, rd, rm, rhs, tid, acc,
    tfield, tsend, bfield, bsend, cyfield, cysend, cc, halo, text, bext, cyx,
    ubuf, gbuf, abuf, rbuf, qbuf, dots, red1, red2,
    s_m, s_w, s_d, r_m, r_w, r_d, s_t, r_t, s_b, r_b, s_c, r_c, s_h, r_h, s_1, r_1, s_2, r_2,
):
    px = lax.axis_index("px")
    py = lax.axis_index("py")

    def ypeer(k):
        return lax.rem(px + k, NPX)

    def opeer(k):
        x = lax.rem(py // 4 + k // 4, 4)
        z = lax.rem(lax.rem(py, 4) + lax.rem(k, 4), 4)
        return x * 4 + z

    barrier = pltpu.get_barrier_semaphore()

    def greet_px(k, carry):
        pl.semaphore_signal(barrier, inc=1, device_id={"px": ypeer(k)}, device_id_type=MESH)
        return carry

    def greet_py(k, carry):
        pl.semaphore_signal(barrier, inc=1, device_id={"py": opeer(k)}, device_id_type=MESH)
        return carry

    lax.fori_loop(1, NPX, greet_px, 0)
    lax.fori_loop(1, NPY, greet_py, 0)

    row = iota((L, L), 0)
    col = iota((L, L), 1)
    owner = own[...]
    hit = jnp.concatenate([(owner == d).astype(f32) for d in range(NPY)], axis=0)
    hit16 = hit.astype(bf16)
    upper = (row < col).astype(f32).astype(bf16)
    before = ((row // 8 == col // 8) & (col < row)).astype(f32).astype(bf16)
    inside = dot(hit16, upper)
    count = dot(hit16, jnp.ones((L, L), bf16))
    keys[...] = jnp.where(hit > 0.5, inside + dot(before, count.astype(bf16)), -1.0)

    share = itp[...]
    s_hi, rest = split(share)
    s_hi = s_hi.astype(f32)
    rest = share - s_hi
    s_mid = rest.astype(bf16).astype(f32)
    s_lo = rest - s_mid
    cell = key[...]
    fx = ((cell // NB) * 16 + sten[...]).astype(f32)
    seg = lax.rem(cell, NB).astype(f32)
    zero = jnp.zeros((3, L), f32)
    for bl in range(8):
        pick = [t[bl:bl + 1, :] for t in (s_hi, s_mid, s_lo, fx, seg)] + [zero]
        metaq[:, bl * L:(bl + 1) * L] = jnp.concatenate(pick, axis=0).astype(bf16)

    def cut(i, carry):
        rows = pl.ds(pl.multiple_of(i * L, L), L)
        w = wgt[rows, :]
        hi, lo = split(w)
        vals[rows, 0:L] = hi
        vals[rows, L:2 * L] = lo
        hi, lo = split(w * inn[rows, :])
        vals[rows, 2 * L:3 * L] = hi
        vals[rows, 3 * L:4 * L] = lo
        return carry

    lax.fori_loop(0, 8, cut, 0)

    rowmask = iota((L, L), 0) < L - 1
    for j in range(2):
        for f in range(2):
            cc[j, f] = cin[f, :, j * L:(j + 1) * L]
        cc[j, 2] = jnp.where(rowmask, cxin[:, j * L:(j + 1) * L], 0.0)
    lanes16 = iota((16, L), 1)
    for b in range(NB):
        tile = cyin[:, b * L:(b + 1) * L]
        if b == NB - 1:
            tile = jnp.where(lanes16 < L - 1, tile, 0.0)
        cyfield[0, b, 0] = tile

    def pack(field, out):
        def one(p, carry):
            out[p, :, 0] = field[:, 2 * p]
            out[p, :, 1] = field[:, 2 * p + 1]
            right = field[:, lax.rem(2 * p + 2, NB)]
            left = field[:, lax.rem(2 * p + NB - 1, NB)]
            out[p, :, 2] = jnp.where(iota(right.shape, right.ndim - 1) < 64, right, left)
            return carry

        lax.fori_loop(0, NPX, one, 0)

    def block(ext, k):
        return ext.at[:, :, :, pl.ds(pl.multiple_of(k * 16, 16), 16), :]

    def turn(send, ext, k, ssem, rsem):
        return pltpu.make_async_remote_copy(
            src_ref=send.at[ypeer(k)], dst_ref=block(ext, px),
            send_sem=ssem.at[k], recv_sem=rsem.at[k],
            device_id={"px": ypeer(k)}, device_id_type=MESH,
        )

    def turned(send, ext, k, ssem, rsem):
        source = lax.rem(px + NPX - k, NPX)
        return pltpu.make_async_remote_copy(
            src_ref=send.at[source], dst_ref=block(ext, source),
            send_sem=ssem.at[k], recv_sem=rsem.at[k],
            device_id={"px": ypeer(k)}, device_id_type=MESH,
        )

    def start_turn(send, ext, ssem, rsem):
        def one(k, carry):
            turn(send, ext, k, ssem, rsem).start()
            return carry

        lax.fori_loop(1, NPX, one, 0)
        ext[:, :, :, pl.ds(pl.multiple_of(px * 16, 16), 16), :] = send[px]

    def end_turn(send, ext, ssem, rsem):
        def one(k, carry):
            turned(send, ext, k, ssem, rsem).wait_recv()
            turn(send, ext, k, ssem, rsem).wait_send()
            return carry

        lax.fori_loop(1, NPX, one, 0)

    pack(cyfield, cysend)

    pl.semaphore_wait(barrier, NPX - 1 + NPY - 1)

    def edge(side):
        peer = ypeer(1 if side == 1 else NPX - 1)
        return pltpu.make_async_remote_copy(
            src_ref=cc.at[side], dst_ref=halo.at[side],
            send_sem=s_h.at[side], recv_sem=r_h.at[side],
            device_id={"px": peer}, device_id_type=MESH,
        )

    edge(0).start()
    edge(1).start()
    start_turn(cysend, cyx, s_c, r_c)

    def route(buf, land, k, ssem, rsem):
        return pltpu.make_async_remote_copy(
            src_ref=buf.at[k], dst_ref=land.at[k],
            send_sem=ssem.at[k], recv_sem=rsem.at[k],
            device_id={"py": opeer(k)}, device_id_type=MESH,
        )

    slot = iota((CAP, L), 0).astype(f32)

    def gather(k):
        base = pl.multiple_of(opeer(k) * 8, 8)
        mine = keys[pl.ds(base, 8), :]
        for bl in range(8):
            pbuf[:, bl * L:(bl + 1) * L] = (slot == mine[bl:bl + 1, :]).astype(f32).astype(bf16)
        meta = lax.dot_general(metaq[...], pbuf[...], NT, preferred_element_type=f32)
        out = dot(pbuf[...], vals[...])
        return meta, out[:, 0:L] + out[:, L:2 * L], out[:, 2 * L:3 * L] + out[:, 3 * L:4 * L]

    def send_rows(k, carry):
        meta, w, wd = gather(k)
        sm[k] = meta
        sw[k] = w
        sd[k] = wd
        route(sm, rm, k, s_m, r_m).start()
        route(sw, rw, k, s_w, r_w).start()
        return carry

    lax.fori_loop(1, NPY, send_rows, 0)

    def send_data(k, carry):
        route(sd, rd, k, s_d, r_d).start()
        return carry

    lax.fori_loop(1, NPY, send_data, 0)
    meta, w, wd = gather(0)
    rm[0] = meta
    rw[0] = w
    rd[0] = wd

    for side in range(2):
        edge(side).wait_recv()
    lanes = iota((L, L), 1)
    for f in range(3):
        cc[2, f] = jnp.where(lanes < 64, halo[0, f], halo[1, f])
    end_turn(cysend, cyx, s_c, r_c)

    last = iota((16, L), 1) == L - 1
    first = iota((16, L), 1) == 0

    def tiles(count, body):
        def one(t, carry):
            body(t // 2, lax.rem(t, 2))
            return carry

        lax.fori_loop(0, count, one, 0)

    def chunks(body):
        def one(i, carry):
            rows = pl.ds(pl.multiple_of(i * 16, 16), 16)
            c = [cyx[0, j, 0, rows, :] for j in range(3)]
            for f in range(2):
                body(f, rows, c)
            return carry

        lax.fori_loop(0, 8, one, 0)

    def first_x(j, f):
        ubuf[j, f] = xsweep(cc[j, f], cc[j, 2])

    def first_y(f, rows, c):
        v = ysweep([ubuf[j, f, rows, :] for j in range(3)], c, last, first)
        for j in range(3):
            ubuf[j, f, rows, :] = v[j]

    tiles(6, first_x)
    chunks(first_y)

    pick = jnp.where(iota((8, L), 0) < 3, 1.0, 0.0).astype(bf16)
    target = iota((T, 4 * CAP), 0).astype(f32)

    def group(g, land, buf, ssem, rsem, with_meta, parts):
        for i in range(4):
            k = 4 * g + i

            @pl.when(k > 0)
            def _():
                if with_meta:
                    route(sm, rm, k, s_m, r_m).wait_recv()
                route(buf, land, k, ssem, rsem).wait_recv()

            meta = rm[k]
            s = lax.dot_general(meta.astype(bf16), pick, TN, preferred_element_type=f32)
            v = land[k]
            va = v * (1.0 - s)
            vs = v * s
            terms = (va * (1.0 - s), vs * s, vs * (1.0 - s)) if parts == 3 else (va, vs)
            rows = slice(i * CAP, (i + 1) * CAP)
            for n, term in enumerate(terms):
                hi, lo = split(term)
                rhs[rows, 2 * n * L:(2 * n + 1) * L] = hi
                rhs[rows, (2 * n + 1) * L:(2 * n + 2) * L] = lo
            tid[0:1, rows] = meta[4:5, :] * 32.0 + meta[3:4, :]
        onehot = (target == tid[0:1, :]).astype(f32).astype(bf16)
        width = 2 * parts * L
        part = dot(onehot, rhs[:, 0:width])

        @pl.when(g == 0)
        def _():
            acc[:, 0:width] = part

        @pl.when(g > 0)
        def _():
            acc[:, 0:width] += part

    def w_group(g, carry):
        group(g, rw, sw, s_w, r_w, True, 3)
        return carry

    lax.fori_loop(0, 4, w_group, 0)

    def column(n):
        return acc[:, 2 * n * L:(2 * n + 1) * L] + acc[:, (2 * n + 1) * L:(2 * n + 2) * L]

    tfield[0] = (column(0) + pltpu.roll(column(1), 1, 0)).reshape(NB, 2, 16, L)
    tfield[1] = column(2).reshape(NB, 2, 16, L)
    pack(tfield, tsend)
    start_turn(tsend, text, s_t, r_t)
    end_turn(tsend, text, s_t, r_t)

    def mid_chunk(f, rows, c):
        u = [ubuf[j, f, rows, :] for j in range(3)]
        v = [tri(u[j], text[0, j, f, rows, :], text[1, j, f, rows, :]) for j in range(3)]
        v = ysweep(v, c, last, first)
        for j in range(3):
            gbuf[j, f, rows, :] = v[j]

    chunks(mid_chunk)

    def image_start(j, f):
        abuf[j, f] = cc[j, f] + xsweep(gbuf[j, f], cc[j, 2])

    tiles(6, image_start)

    def d_group(g, carry):
        group(g, rd, sd, s_d, r_d, False, 2)
        return carry

    lax.fori_loop(0, 4, d_group, 0)
    bfield[0] = (column(0) + pltpu.roll(column(1), 1, 0)).reshape(NB, 2, 16, L)
    pack(bfield, bsend)
    start_turn(bsend, bext, s_b, r_b)
    end_turn(bsend, bext, s_b, r_b)

    dots[...] = jnp.zeros_like(dots)

    def add_dot(n, a, b):
        dots[n] += jnp.sum((a * b).reshape(16, 8, L), axis=0)

    def b_chunk(f, rows, c):
        v = ysweep([bext[0, j, f, rows, :] for j in range(3)], c, last, first)
        for j in range(3):
            gbuf[j, f, rows, :] = v[j]

    chunks(b_chunk)

    def residual_tile(j, f):
        r = xsweep(gbuf[j, f], cc[j, 2]) - abuf[j, f]
        rbuf[j, f] = r

        @pl.when(j < 2)
        def _():
            add_dot(0, r, r)

        ubuf[j, f] = xsweep(r, cc[j, 2])

    tiles(6, residual_tile)

    def full_chunk(f, rows, c):
        u = ysweep([ubuf[j, f, rows, :] for j in range(3)], c, last, first)
        v = [tri(u[j], text[0, j, f, rows, :], text[1, j, f, rows, :]) for j in range(3)]
        v = ysweep(v, c, last, first)
        for j in range(3):
            gbuf[j, f, rows, :] = v[j]

    chunks(full_chunk)

    def q_tile(j, f):
        r = rbuf[j, f]
        q = r + xsweep(gbuf[j, f], cc[j, 2])
        qbuf[j, f] = q

        @pl.when(j < 2)
        def _():
            add_dot(1, r, q)
            add_dot(2, q, q)

        ubuf[j, f] = xsweep(q, cc[j, 2])

    tiles(6, q_tile)
    chunks(full_chunk)

    def p_tile(j, f):
        q = qbuf[j, f]
        p = q + xsweep(gbuf[j, f], cc[j, 2])
        abuf[j, f] = p
        add_dot(3, q, p)

    tiles(4, p_tile)

    lines = [jnp.sum(dots[n], axis=0, keepdims=True) for n in range(4)]
    red1[0] = jnp.concatenate(lines + [jnp.zeros((4, L), f32)], axis=0)

    def sum1(k):
        return pltpu.make_async_remote_copy(
            src_ref=red1.at[0], dst_ref=red1.at[k], send_sem=s_1.at[k], recv_sem=r_1.at[k],
            device_id={"px": ypeer(k)}, device_id_type=MESH,
        )

    def sum2(k):
        return pltpu.make_async_remote_copy(
            src_ref=red2.at[0], dst_ref=red2.at[k], send_sem=s_2.at[k], recv_sem=r_2.at[k],
            device_id={"py": opeer(k)}, device_id_type=MESH,
        )

    for k in range(1, NPX):
        sum1(k).start()
    for k in range(1, NPX):
        sum1(k).wait_recv()
    total = red1[0]
    for k in range(1, NPX):
        total = total + red1[k]
    red2[0] = total
    for k in range(1, NPY):
        sum2(k).start()
    for k in range(1, NPY):
        sum2(k).wait_recv()
    total = red2[0]
    for k in range(1, NPY):
        total = total + red2[k]
    sums = jnp.sum(total, axis=1, keepdims=True)
    rr, rq, qq, qp = [sums[n:n + 1, :] for n in range(4)]
    alpha = rr / rq
    new = alpha * (alpha * qq) - rr
    beta = new / rr
    grow = 1.0 + beta
    alpha2 = new / (grow * grow * rq - 2.0 * alpha * grow * qq + alpha * alpha * qp)
    kr = alpha + alpha2 * grow
    kq = -alpha2 * alpha

    for j in range(2):
        for f in range(2):
            r = rbuf[j, f]
            q = qbuf[j, f]
            ctl[f, :, j * L:(j + 1) * L] = cc[j, f] + kr * r + kq * q
            res[f, :, j * L:(j + 1) * L] = r - kr * q - kq * abuf[j, f]

    for side in range(2):
        edge(side).wait_send()

    def drain_px(k, carry):
        sum1(k).wait_send()
        return carry

    def drain_py(k, carry):
        route(sm, rm, k, s_m, r_m).wait_send()
        route(sw, rw, k, s_w, r_w).wait_send()
        route(sd, rd, k, s_d, r_d).wait_send()
        sum2(k).wait_send()
        return carry

    lax.fori_loop(1, NPX, drain_px, 0)
    lax.fori_loop(1, NPY, drain_py, 0)


def shards(control_start, coef_x, coef_y, innovation, obs_weight, interp, obs_owner, cell_key, stencil):
    dma = pltpu.SemaphoreType.DMA
    vm = pltpu.VMEM
    field = vm((3, 2, L, L), f32)
    scratch = [
        vm((L, L), f32), vm((ROWS, 4 * L), bf16), vm((8, ROWS), bf16), vm((CAP, ROWS), bf16),
        vm((NPY, CAP, L), f32), vm((NPY, CAP, L), f32), vm((NPY, 8, CAP), f32),
        vm((NPY, CAP, L), f32), vm((NPY, CAP, L), f32), vm((NPY, 8, CAP), f32),
        vm((4 * CAP, 6 * L), bf16), vm((8, 4 * CAP), f32), vm((T, 6 * L), f32),
        vm((2, NB, 2, 16, L), f32), vm((NPX, 2, 3, 2, 16, L), f32),
        vm((1, NB, 2, 16, L), f32), vm((NPX, 1, 3, 2, 16, L), f32),
        vm((1, NB, 1, 16, L), f32), vm((NPX, 1, 3, 1, 16, L), f32),
        vm((3, 3, L, L), f32), vm((2, 3, L, L), f32),
        vm((2, 3, 2, L, L), f32), vm((1, 3, 2, L, L), f32), vm((1, 3, 1, L, L), f32),
        field, field, field, field, field,
        vm((4, 8, L), f32), vm((NPX, 8, L), f32), vm((NPY, 8, L), f32),
        dma((NPY,)), dma((NPY,)), dma((NPY,)), dma((NPY,)), dma((NPY,)), dma((NPY,)),
        dma((NPX,)), dma((NPX,)), dma((NPX,)), dma((NPX,)), dma((NPX,)), dma((NPX,)),
        dma((2,)), dma((2,)), dma((NPX,)), dma((NPX,)), dma((NPY,)), dma((NPY,)),
    ]
    out = jax.ShapeDtypeStruct((2, L, 2 * L), f32)
    control, residual = pl.pallas_call(
        kernel,
        out_shape=(out, out),
        in_specs=[pl.BlockSpec(memory_space=pltpu.VMEM)] * 9,
        out_specs=(pl.BlockSpec(memory_space=pltpu.VMEM),) * 2,
        scratch_shapes=scratch,
        compiler_params=pltpu.CompilerParams(
            collective_id=0, has_side_effects=True, vmem_limit_bytes=48 * 1024 * 1024
        ),
        name="assimilate",
    )(
        obs_owner.reshape(8, L), cell_key.reshape(8, L), stencil.reshape(8, L), interp.reshape(8, L),
        innovation, obs_weight, control_start.reshape(2, L, 2 * L), coef_x.reshape(L, 2 * L),
        coef_y.reshape(16, NB * L),
    )
    shape = control_start.shape
    return control.reshape(shape), residual.reshape(shape)


def solution(mesh):
    return jax.shard_map(
        shards,
        mesh=mesh,
        in_specs=(
            P(None, "py", None, "px"),
            P("py", None, "px"),
            P("py", "px", None),
            P(("px", "py"), None),
            P(("px", "py"), None),
            P(("px", "py")),
            P(("px", "py"), None),
            P(("px", "py")),
            P(("px", "py")),
        ),
        out_specs=(P(None, "py", None, "px"), P(None, "py", None, "px")),
        check_vma=False,
    )
```

```python
import jax
import jax.numpy as jnp
from jax import lax
from jax.experimental import pallas as pl
from jax.experimental.pallas import tpu as pltpu
from jax.sharding import PartitionSpec as P

NPX = 8
NPY = 16
CAP = 192
ROWS = 1024
L = 128
M = 4
NB = 16
T = 512
f32 = jnp.float32
bf16 = jnp.bfloat16
MESH = pl.DeviceIdType.MESH
NT = (((1,), (1,)), ((), ()))
TN = (((0,), (0,)), ((), ()))


def dot(a, b):
    return jnp.dot(a, b, preferred_element_type=f32)


def iota(shape, axis):
    return lax.broadcasted_iota(jnp.int32, shape, axis)


def split(v):
    hi = v.astype(bf16)
    return hi, (v - hi.astype(f32)).astype(bf16)


def xshift(v, k):
    return [pltpu.roll(t, (-k) % L, 0) for t in v] if k else v


def yshift(v, k):
    if k == 0:
        return v
    lane = iota(v[0].shape, 1)
    r = [pltpu.roll(t, (-k) % L, 1) for t in v]
    n = len(v)
    if k > 0:
        return [jnp.where(lane < L - k, r[j], r[(j + 1) % n]) for j in range(n)]
    return [jnp.where(lane >= -k, r[j], r[(j + n - 1) % n]) for j in range(n)]


def mul(a, b):
    return [x * y for x, y in zip(a, b)]


def add(*terms):
    total = terms[0]
    for t in terms[1:]:
        total = [x + y for x, y in zip(total, t)]
    return total


def band(c, shift):
    a = shift(c, -1)
    d = [1.0 - x - y for x, y in zip(c, a)]
    p0 = add(mul(d, d), mul(c, c), mul(a, a))
    p1 = mul(c, add(d, shift(d, 1)))
    p2 = mul(c, shift(c, 1))
    n1, n2 = shift(p1, -1), shift(p2, -2)
    up1 = shift(p1, 1)
    b0 = add(mul(p0, p0), mul(p1, p1), mul(p2, p2), mul(n1, n1), mul(n2, n2))
    b1 = add(mul(p1, add(p0, shift(p0, 1))), mul(p2, up1), mul(n1, shift(p2, -1)))
    b2 = add(mul(p0, p2), mul(p1, up1), mul(p2, shift(p0, 2)))
    b3 = add(mul(p1, shift(p2, 1)), mul(p2, shift(p1, 2)))
    b4 = mul(p2, shift(p2, 2))
    return [shift(b4, -4), shift(b3, -3), shift(b2, -2), shift(b1, -1), b0, b1, b2, b3, b4]


def sweep(w, v, shift, keep=3):
    total = None
    for m in range(2 * M + 1):
        moved = shift(v, m - M)[:keep]
        term = [w(m, j) * t for j, t in enumerate(moved)]
        total = term if total is None else add(total, term)
    return total


def tri(u, d, e):
    eu = e * u
    return d * u + e * pltpu.roll(u, u.shape[0] - 1, 0) + pltpu.roll(eu, 1, 0)


def kernel(
    h_own, h_key, h_sten, h_itp, h_inn, h_wgt, h_c, h_cx, h_cy, ctl, res,
    own, key, sten, itp, inn, wgt, cyin, s_in, wx, wy,
    keys, vals, metaq, pbuf, sw, sd, sm, rw, rd, rm, rhs, tid, acc,
    tfield, tsend, bfield, bsend, cyfield, cysend, cc, halo, text, bext, cyx,
    ubuf, gbuf, abuf, rbuf, qbuf, dots, red1, red2,
    s_m, s_w, s_d, r_m, r_w, r_d, s_t, r_t, s_b, r_b, s_c, r_c, s_h, r_h, s_1, r_1, s_2, r_2,
):
    px = lax.axis_index("px")
    py = lax.axis_index("py")

    def ypeer(k):
        return lax.rem(px + k, NPX)

    def opeer(k):
        x = lax.rem(py // 4 + lax.rem(k, 4), 4)
        z = lax.rem(lax.rem(py, 4) + k // 4 + 4 - lax.rem(k, 4), 4)
        return x * 4 + z

    loads = [(h_own, own), (h_key, key), (h_sten, sten), (h_itp, itp), (h_wgt, wgt), (h_inn, inn), (h_cy, cyin)]
    for j in range(2):
        lanes = slice(j * L, (j + 1) * L)
        loads.append((h_c.at[:, :, lanes], cc.at[j, 0:2]))
        loads.append((h_cx.at[:, lanes], cc.at[j, 2]))
    loads = [pltpu.make_async_copy(a, b, s_in.at[n]) for n, (a, b) in enumerate(loads)]
    for load in loads:
        load.start()

    barrier = pltpu.get_barrier_semaphore()

    def greet_px(k, carry):
        pl.semaphore_signal(barrier, inc=1, device_id={"px": ypeer(k)}, device_id_type=MESH)
        return carry

    def greet_py(k, carry):
        pl.semaphore_signal(barrier, inc=1, device_id={"py": opeer(k)}, device_id_type=MESH)
        return carry

    lax.fori_loop(1, NPX, greet_px, 0)
    lax.fori_loop(1, NPY, greet_py, 0)

    for n in range(4):
        loads[n].wait()
    row = iota((L, L), 0)
    col = iota((L, L), 1)
    owner = own[...]
    hit = jnp.concatenate([(owner == d).astype(f32) for d in range(NPY)], axis=0)
    hit16 = hit.astype(bf16)
    upper = (row < col).astype(f32).astype(bf16)
    before = ((row // 8 == col // 8) & (col < row)).astype(f32).astype(bf16)
    inside = dot(hit16, upper)
    count = dot(hit16, jnp.ones((L, L), bf16))
    keys[...] = jnp.where(hit > 0.5, inside + dot(before, count.astype(bf16)), -1.0)

    share = itp[...]
    s_hi, rest = split(share)
    s_hi = s_hi.astype(f32)
    rest = share - s_hi
    s_mid = rest.astype(bf16).astype(f32)
    s_lo = rest - s_mid
    cell = key[...]
    fx = ((cell // NB) * 16 + sten[...]).astype(f32)
    seg = lax.rem(cell, NB).astype(f32)
    zero = jnp.zeros((3, L), f32)
    for bl in range(8):
        pick = [t[bl:bl + 1, :] for t in (s_hi, s_mid, s_lo, fx, seg)] + [zero]
        metaq[:, bl * L:(bl + 1) * L] = jnp.concatenate(pick, axis=0).astype(bf16)

    loads[4].wait()
    loads[5].wait()

    def cut(i, carry):
        rows = pl.ds(pl.multiple_of(i * L, L), L)
        w = wgt[rows, :]
        hi, lo = split(w)
        vals[rows, 0:L] = hi
        vals[rows, L:2 * L] = lo
        hi, lo = split(w * inn[rows, :])
        vals[rows, 2 * L:3 * L] = hi
        vals[rows, 3 * L:4 * L] = lo
        return carry

    lax.fori_loop(0, 8, cut, 0)

    for load in loads[6:]:
        load.wait()
    for j in range(2):
        tail = cc[j, 2, L - 8:L, :]
        cc[j, 2, L - 8:L, :] = jnp.where(iota((8, L), 0) < 7, tail, 0.0)
    lanes16 = iota((16, L), 1)
    for b in range(NB):
        tile = cyin[:, b * L:(b + 1) * L]
        if b == NB - 1:
            tile = jnp.where(lanes16 < L - 1, tile, 0.0)
        cyfield[0, b, 0] = tile

    def pack(field, out):
        def one(p, carry):
            out[p, :, 0] = field[:, 2 * p]
            out[p, :, 1] = field[:, 2 * p + 1]
            right = field[:, lax.rem(2 * p + 2, NB)]
            left = field[:, lax.rem(2 * p + NB - 1, NB)]
            out[p, :, 2] = jnp.where(iota(right.shape, right.ndim - 1) < 64, right, left)
            return carry

        lax.fori_loop(0, NPX, one, 0)

    def block(ext, k):
        return ext.at[:, :, :, pl.ds(pl.multiple_of(k * 16, 16), 16), :]

    def turn(send, ext, k, ssem, rsem):
        return pltpu.make_async_remote_copy(
            src_ref=send.at[ypeer(k)], dst_ref=block(ext, px),
            send_sem=ssem.at[k], recv_sem=rsem.at[k],
            device_id={"px": ypeer(k)}, device_id_type=MESH,
        )

    def turned(send, ext, k, ssem, rsem):
        source = lax.rem(px + NPX - k, NPX)
        return pltpu.make_async_remote_copy(
            src_ref=send.at[source], dst_ref=block(ext, source),
            send_sem=ssem.at[k], recv_sem=rsem.at[k],
            device_id={"px": ypeer(k)}, device_id_type=MESH,
        )

    def start_turn(send, ext, ssem, rsem):
        def one(k, carry):
            turn(send, ext, k, ssem, rsem).start()
            return carry

        lax.fori_loop(1, NPX, one, 0)
        ext[:, :, :, pl.ds(pl.multiple_of(px * 16, 16), 16), :] = send[px]

    def end_turn(send, ext, ssem, rsem):
        def one(k, carry):
            turned(send, ext, k, ssem, rsem).wait_recv()
            turn(send, ext, k, ssem, rsem).wait_send()
            return carry

        lax.fori_loop(1, NPX, one, 0)

    pack(cyfield, cysend)

    pl.semaphore_wait(barrier, NPX - 1 + NPY - 1)

    def edge(side):
        peer = ypeer(1 if side == 1 else NPX - 1)
        return pltpu.make_async_remote_copy(
            src_ref=cc.at[side], dst_ref=halo.at[side],
            send_sem=s_h.at[side], recv_sem=r_h.at[side],
            device_id={"px": peer}, device_id_type=MESH,
        )

    edge(0).start()
    edge(1).start()
    start_turn(cysend, cyx, s_c, r_c)

    def route(buf, land, k, ssem, rsem):
        return pltpu.make_async_remote_copy(
            src_ref=buf.at[k], dst_ref=land.at[k],
            send_sem=ssem.at[k], recv_sem=rsem.at[k],
            device_id={"py": opeer(k)}, device_id_type=MESH,
        )

    slot = iota((CAP, L), 0).astype(f32)

    def gather(k):
        base = pl.multiple_of(opeer(k) * 8, 8)
        mine = keys[pl.ds(base, 8), :]
        for bl in range(8):
            pbuf[:, bl * L:(bl + 1) * L] = (slot == mine[bl:bl + 1, :]).astype(f32).astype(bf16)
        meta = lax.dot_general(metaq[...], pbuf[...], NT, preferred_element_type=f32)
        out = dot(pbuf[...], vals[...])
        return meta, out[:, 0:L] + out[:, L:2 * L], out[:, 2 * L:3 * L] + out[:, 3 * L:4 * L]

    def send_rows(k, carry):
        meta, w, wd = gather(k)
        sm[k] = meta
        sw[k] = w
        sd[k] = wd
        route(sm, rm, k, s_m, r_m).start()
        route(sw, rw, k, s_w, r_w).start()
        return carry

    lax.fori_loop(1, NPY, send_rows, 0)

    meta, w, wd = gather(0)
    rm[0] = meta
    rw[0] = w
    rd[0] = wd

    for side in range(2):
        edge(side).wait_recv()
    lanes = iota((L, L), 1)
    for f in range(3):
        cc[2, f] = jnp.where(lanes < 64, halo[0, f], halo[1, f])
    end_turn(cysend, cyx, s_c, r_c)

    CH = 32

    def tiles(count, body):
        def one(j, carry):
            for f in range(2):
                body(j, f)
            return carry

        lax.fori_loop(0, count, one, 0)

    def chunks(body):
        def one(i, carry):
            rows = pl.ds(pl.multiple_of(i * CH, CH), CH)
            for f in range(2):
                body(f, rows)
            return carry

        lax.fori_loop(0, L // CH, one, 0)

    def bands_x(j, carry):
        for m, w in enumerate(band([cc[j, 2]], xshift)):
            wx[m, j] = w[0]
        return carry

    def bands_y(i, carry):
        rows = pl.ds(pl.multiple_of(i * 16, 16), 16)
        for m, w in enumerate(band([cyx[0, j, 0, rows, :] for j in range(3)], yshift)):
            for j in range(3):
                wy[m, j, rows, :] = w[j]
        return carry

    lax.fori_loop(0, 3, bands_x, 0)
    lax.fori_loop(0, 8, bands_y, 0)

    def sweep_x(v, j):
        return sweep(lambda m, _: wx[m, j], [v], xshift)[0]

    def sweep_y(v, rows, keep=3):
        return sweep(lambda m, j: wy[m, j, rows, :], v, yshift, keep)

    def first_x(j, f):
        ubuf[j, f] = sweep_x(cc[j, f], j)

    def first_y(f, rows):
        v = sweep_y([ubuf[j, f, rows, :] for j in range(3)], rows)
        for j in range(3):
            ubuf[j, f, rows, :] = v[j]

    tiles(3, first_x)
    chunks(first_y)

    def send_data(k, carry):
        route(sw, rw, k, s_w, r_w).wait_send()
        route(sd, rd, k, s_d, r_d).start()
        return carry

    lax.fori_loop(1, NPY, send_data, 0)

    pick = jnp.where(iota((8, L), 0) < 3, 1.0, 0.0).astype(bf16)
    target = iota((T, 4 * CAP), 0).astype(f32)

    def group(g, land, buf, ssem, rsem, with_meta, parts):
        for i in range(4):
            k = 4 * g + i

            @pl.when(k > 0)
            def _():
                if with_meta:
                    route(sm, rm, k, s_m, r_m).wait_recv()
                route(buf, land, k, ssem, rsem).wait_recv()

            meta = rm[k]
            s = lax.dot_general(meta.astype(bf16), pick, TN, preferred_element_type=f32)
            v = land[k]
            va = v * (1.0 - s)
            vs = v * s
            terms = (va * (1.0 - s), vs * s, vs * (1.0 - s)) if parts == 3 else (va, vs)
            rows = slice(i * CAP, (i + 1) * CAP)
            for n, term in enumerate(terms):
                hi, lo = split(term)
                rhs[rows, 2 * n * L:(2 * n + 1) * L] = hi
                rhs[rows, (2 * n + 1) * L:(2 * n + 2) * L] = lo
            tid[0:1, rows] = meta[4:5, :] * 32.0 + meta[3:4, :]
        onehot = (target == tid[0:1, :]).astype(f32).astype(bf16)
        width = 2 * parts * L
        part = dot(onehot, rhs[:, 0:width])

        @pl.when(g == 0)
        def _():
            acc[:, 0:width] = part

        @pl.when(g > 0)
        def _():
            acc[:, 0:width] += part

    def w_group(g, carry):
        group(g, rw, sw, s_w, r_w, True, 3)
        return carry

    lax.fori_loop(0, 4, w_group, 0)

    def column(n):
        return acc[:, 2 * n * L:(2 * n + 1) * L] + acc[:, (2 * n + 1) * L:(2 * n + 2) * L]

    tfield[0] = (column(0) + pltpu.roll(column(1), 1, 0)).reshape(NB, 2, 16, L)
    tfield[1] = column(2).reshape(NB, 2, 16, L)
    pack(tfield, tsend)
    start_turn(tsend, text, s_t, r_t)

    def d_group(g, carry):
        group(g, rd, sd, s_d, r_d, False, 2)
        return carry

    lax.fori_loop(0, 1, d_group, 0)
    end_turn(tsend, text, s_t, r_t)

    def spread(f, rows, keep=3):
        u = [ubuf[j, f, rows, :] for j in range(3)]
        return u, [tri(u[j], text[0, j, f, rows, :], text[1, j, f, rows, :]) for j in range(3)]

    def mid_chunk(f, rows):
        v = sweep_y(spread(f, rows)[1], rows)
        for j in range(3):
            gbuf[j, f, rows, :] = v[j]

    chunks(mid_chunk)

    def image_start(j, f):
        abuf[j, f] = cc[j, f] + sweep_x(gbuf[j, f], j)

    tiles(3, image_start)
    lax.fori_loop(1, 4, d_group, 0)
    bfield[0] = (column(0) + pltpu.roll(column(1), 1, 0)).reshape(NB, 2, 16, L)
    pack(bfield, bsend)
    start_turn(bsend, bext, s_b, r_b)
    end_turn(bsend, bext, s_b, r_b)

    dots[...] = jnp.zeros_like(dots)

    def add_dot(n, a, b):
        dots[n] += jnp.sum((a * b).reshape(-1, 8, L), axis=0)

    def b_chunk(f, rows):
        v = sweep_y([bext[0, j, f, rows, :] for j in range(3)], rows)
        for j in range(3):
            gbuf[j, f, rows, :] = v[j]

    chunks(b_chunk)

    def residual_tile(j, f):
        r = sweep_x(gbuf[j, f], j) - abuf[j, f]
        rbuf[j, f] = r

        @pl.when(j < 2)
        def _():
            add_dot(0, r, r)

        ubuf[j, f] = sweep_x(r, j)

    tiles(3, residual_tile)

    def q_chunk(f, rows):
        u = sweep_y([ubuf[j, f, rows, :] for j in range(3)], rows)
        v = [tri(u[j], text[0, j, f, rows, :], text[1, j, f, rows, :]) for j in range(3)]
        for j in range(2):
            add_dot(1, u[j], v[j])
        v = sweep_y(v, rows)
        for j in range(3):
            gbuf[j, f, rows, :] = v[j]

    chunks(q_chunk)

    def q_tile(j, f):
        q = rbuf[j, f] + sweep_x(gbuf[j, f], j)
        qbuf[j, f] = q

        @pl.when(j < 2)
        def _():
            add_dot(2, q, q)

        ubuf[j, f] = sweep_x(q, j)

    tiles(3, q_tile)

    def p_up(f, rows):
        u = sweep_y([ubuf[j, f, rows, :] for j in range(3)], rows)
        v = [tri(u[j], text[0, j, f, rows, :], text[1, j, f, rows, :]) for j in range(3)]
        for j in range(2):
            add_dot(3, u[j], v[j])
        for j in range(3):
            ubuf[j, f, rows, :] = v[j]

    chunks(p_up)

    def p_down(f, rows):
        v = sweep_y([ubuf[j, f, rows, :] for j in range(3)], rows, 2)
        for j in range(2):
            gbuf[j, f, rows, :] = v[j]

    def p_tile(j, f):
        abuf[j, f] = qbuf[j, f] + sweep_x(gbuf[j, f], j)

    lines = [jnp.sum(dots[n], axis=0, keepdims=True) for n in range(4)]
    red1[0] = jnp.concatenate(lines + [jnp.zeros((4, L), f32)], axis=0)

    def sum1(k):
        return pltpu.make_async_remote_copy(
            src_ref=red1.at[0], dst_ref=red1.at[k], send_sem=s_1.at[k], recv_sem=r_1.at[k],
            device_id={"px": ypeer(k)}, device_id_type=MESH,
        )

    def sum2(k):
        return pltpu.make_async_remote_copy(
            src_ref=red2.at[0], dst_ref=red2.at[k], send_sem=s_2.at[k], recv_sem=r_2.at[k],
            device_id={"py": opeer(k)}, device_id_type=MESH,
        )

    for k in range(1, NPX):
        sum1(k).start()
    chunks(p_down)
    for k in range(1, NPX):
        sum1(k).wait_recv()
    total = red1[0]
    for k in range(1, NPX):
        total = total + red1[k]
    red2[0] = total
    for k in range(1, NPY):
        sum2(k).start()
    tiles(2, p_tile)
    for k in range(1, NPY):
        sum2(k).wait_recv()
    total = red2[0]
    for k in range(1, NPY):
        total = total + red2[k]
    sums = jnp.sum(total, axis=1, keepdims=True)
    rr, gain, qq, gain2 = [sums[n:n + 1, :] for n in range(4)]
    rq = rr + gain
    qp = qq + gain2
    alpha = rr / rq
    new = alpha * (alpha * qq) - rr
    beta = new / rr
    grow = 1.0 + beta
    alpha2 = new / (grow * grow * rq - 2.0 * alpha * grow * qq + alpha * alpha * qp)
    kr = alpha + alpha2 * grow
    kq = -alpha2 * alpha

    for j in range(2):
        for f in range(2):
            r = rbuf[j, f]
            q = qbuf[j, f]
            ctl[f, :, j * L:(j + 1) * L] = cc[j, f] + kr * r + kq * q
            res[f, :, j * L:(j + 1) * L] = r - kr * q - kq * abuf[j, f]

    for side in range(2):
        edge(side).wait_send()

    def drain_px(k, carry):
        sum1(k).wait_send()
        return carry

    def drain_py(k, carry):
        route(sm, rm, k, s_m, r_m).wait_send()
        route(sd, rd, k, s_d, r_d).wait_send()
        sum2(k).wait_send()
        return carry

    lax.fori_loop(1, NPX, drain_px, 0)
    lax.fori_loop(1, NPY, drain_py, 0)


def shards(control_start, coef_x, coef_y, innovation, obs_weight, interp, obs_owner, cell_key, stencil):
    dma = pltpu.SemaphoreType.DMA
    vm = pltpu.VMEM
    field = vm((3, 2, L, L), f32)
    scratch = [
        vm((8, L), jnp.int32), vm((8, L), jnp.int32), vm((8, L), jnp.int32), vm((8, L), f32),
        vm((ROWS, L), f32), vm((ROWS, L), f32), vm((16, NB * L), f32), dma((11,)),
        vm((2 * M + 1, 3, L, L), f32), vm((2 * M + 1, 3, L, L), f32),
        vm((L, L), f32), vm((ROWS, 4 * L), bf16), vm((8, ROWS), bf16), vm((CAP, ROWS), bf16),
        vm((NPY, CAP, L), f32), vm((NPY, CAP, L), f32), vm((NPY, 8, CAP), f32),
        vm((NPY, CAP, L), f32), vm((NPY, CAP, L), f32), vm((NPY, 8, CAP), f32),
        vm((4 * CAP, 6 * L), bf16), vm((8, 4 * CAP), f32), vm((T, 6 * L), f32),
        vm((2, NB, 2, 16, L), f32), vm((NPX, 2, 3, 2, 16, L), f32),
        vm((1, NB, 2, 16, L), f32), vm((NPX, 1, 3, 2, 16, L), f32),
        vm((1, NB, 1, 16, L), f32), vm((NPX, 1, 3, 1, 16, L), f32),
        vm((3, 3, L, L), f32), vm((2, 3, L, L), f32),
        vm((2, 3, 2, L, L), f32), vm((1, 3, 2, L, L), f32), vm((1, 3, 1, L, L), f32),
        field, field, field, field, field,
        vm((4, 8, L), f32), vm((NPX, 8, L), f32), vm((NPY, 8, L), f32),
        dma((NPY,)), dma((NPY,)), dma((NPY,)), dma((NPY,)), dma((NPY,)), dma((NPY,)),
        dma((NPX,)), dma((NPX,)), dma((NPX,)), dma((NPX,)), dma((NPX,)), dma((NPX,)),
        dma((2,)), dma((2,)), dma((NPX,)), dma((NPX,)), dma((NPY,)), dma((NPY,)),
    ]
    out = jax.ShapeDtypeStruct((2, L, 2 * L), f32)
    control, residual = pl.pallas_call(
        kernel,
        out_shape=(out, out),
        in_specs=[pl.BlockSpec(memory_space=pltpu.HBM)] * 9,
        out_specs=(pl.BlockSpec(memory_space=pltpu.VMEM),) * 2,
        scratch_shapes=scratch,
        compiler_params=pltpu.CompilerParams(
            collective_id=0, has_side_effects=True, vmem_limit_bytes=60 * 1024 * 1024
        ),
        name="assimilate",
    )(
        obs_owner.reshape(8, L), cell_key.reshape(8, L), stencil.reshape(8, L), interp.reshape(8, L),
        innovation, obs_weight, control_start.reshape(2, L, 2 * L), coef_x.reshape(L, 2 * L),
        coef_y.reshape(16, NB * L),
    )
    shape = control_start.shape
    return control.reshape(shape), residual.reshape(shape)


def solution(mesh):
    return jax.shard_map(
        shards,
        mesh=mesh,
        in_specs=(
            P(None, "py", None, "px"),
            P("py", None, "px"),
            P("py", "px", None),
            P(("px", "py"), None),
            P(("px", "py"), None),
            P(("px", "py")),
            P(("px", "py"), None),
            P(("px", "py")),
            P(("px", "py")),
        ),
        out_specs=(P(None, "py", None, "px"), P(None, "py", None, "px")),
        check_vma=False,
    )
```

```python
import jax
import jax.numpy as jnp
from jax import lax
from jax.experimental import pallas as pl
from jax.experimental.pallas import tpu as pltpu
from jax.sharding import PartitionSpec as P

NPX = 8
NPY = 16
CAP = 192
ROWS = 1024
L = 128
M = 4
NB = 16
T = 512
f32 = jnp.float32
bf16 = jnp.bfloat16
MESH = pl.DeviceIdType.MESH
NT = (((1,), (1,)), ((), ()))
TN = (((0,), (0,)), ((), ()))


def dot(a, b):
    return jnp.dot(a, b, preferred_element_type=f32)


def iota(shape, axis):
    return lax.broadcasted_iota(jnp.int32, shape, axis)


def split(v):
    hi = v.astype(bf16)
    return hi, (v - hi.astype(f32)).astype(bf16)


def xshift(v, k):
    return [pltpu.roll(t, (-k) % L, 0) for t in v] if k else v


def yshift(v, k):
    if k == 0:
        return v
    lane = iota(v[0].shape, 1)
    r = [pltpu.roll(t, (-k) % L, 1) for t in v]
    n = len(v)
    if k > 0:
        return [jnp.where(lane < L - k, r[j], r[(j + 1) % n]) for j in range(n)]
    return [jnp.where(lane >= -k, r[j], r[(j + n - 1) % n]) for j in range(n)]


def mul(a, b):
    return [x * y for x, y in zip(a, b)]


def add(*terms):
    total = terms[0]
    for t in terms[1:]:
        total = [x + y for x, y in zip(total, t)]
    return total


def band(c, shift):
    a = shift(c, -1)
    d = [1.0 - x - y for x, y in zip(c, a)]
    p0 = add(mul(d, d), mul(c, c), mul(a, a))
    p1 = mul(c, add(d, shift(d, 1)))
    p2 = mul(c, shift(c, 1))
    n1, n2 = shift(p1, -1), shift(p2, -2)
    up1 = shift(p1, 1)
    b0 = add(mul(p0, p0), mul(p1, p1), mul(p2, p2), mul(n1, n1), mul(n2, n2))
    b1 = add(mul(p1, add(p0, shift(p0, 1))), mul(p2, up1), mul(n1, shift(p2, -1)))
    b2 = add(mul(p0, p2), mul(p1, up1), mul(p2, shift(p0, 2)))
    b3 = add(mul(p1, shift(p2, 1)), mul(p2, shift(p1, 2)))
    b4 = mul(p2, shift(p2, 2))
    return [shift(b4, -4), shift(b3, -3), shift(b2, -2), shift(b1, -1), b0, b1, b2, b3, b4]


def sweep(w, v, shift, keep=3):
    total = None
    for m in range(2 * M + 1):
        moved = shift(v, m - M)[:keep]
        term = [w(m, j) * t for j, t in enumerate(moved)]
        total = term if total is None else add(total, term)
    return total


def tri(u, d, e):
    eu = e * u
    return d * u + e * pltpu.roll(u, u.shape[0] - 1, 0) + pltpu.roll(eu, 1, 0)


def kernel(
    h_own, h_key, h_sten, h_itp, h_inn, h_wgt, h_c, h_cx, h_cy, ctl, res,
    own, key, sten, itp, inn, wgt, cyin, s_in, wx, wy,
    keys, vals, metaq, pbuf, sw, sd, sm, rw, rd, rm, rhs, tid, acc,
    tfield, tsend, bfield, bsend, cyfield, cysend, cc, halo, text, bext, cyx,
    ubuf, gbuf, abuf, rbuf, qbuf, dots, red1, red2,
    s_m, s_w, s_d, r_m, r_w, r_d, s_t, r_t, s_b, r_b, s_c, r_c, s_h, r_h, s_1, r_1, s_2, r_2,
):
    px = lax.axis_index("px")
    py = lax.axis_index("py")

    def ypeer(k):
        return lax.rem(px + k, NPX)

    def opeer(k):
        k = lax.rem(k + lax.rem(px, 2) * (2 * NPY - 2 * k), NPY)
        x = lax.rem(py // 4 + lax.rem(k, 4), 4)
        z = lax.rem(lax.rem(py, 4) + k // 4 + 4 - lax.rem(k, 4), 4)
        return x * 4 + z

    loads = [(h_own, own), (h_key, key), (h_sten, sten), (h_itp, itp), (h_wgt, wgt), (h_inn, inn), (h_cy, cyin)]
    for j in range(2):
        lanes = slice(j * L, (j + 1) * L)
        loads.append((h_c.at[:, :, lanes], cc.at[j, 0:2]))
        loads.append((h_cx.at[:, lanes], cc.at[j, 2]))
    loads = [pltpu.make_async_copy(a, b, s_in.at[n]) for n, (a, b) in enumerate(loads)]
    for load in loads:
        load.start()

    barrier = pltpu.get_barrier_semaphore()

    def greet_px(k, carry):
        pl.semaphore_signal(barrier, inc=1, device_id={"px": ypeer(k)}, device_id_type=MESH)
        return carry

    def greet_py(k, carry):
        pl.semaphore_signal(barrier, inc=1, device_id={"py": opeer(k)}, device_id_type=MESH)
        return carry

    lax.fori_loop(1, NPX, greet_px, 0)
    lax.fori_loop(1, NPY, greet_py, 0)

    for n in range(4):
        loads[n].wait()
    row = iota((L, L), 0)
    col = iota((L, L), 1)
    owner = own[...]
    hit = jnp.concatenate([(owner == d).astype(f32) for d in range(NPY)], axis=0)
    hit16 = hit.astype(bf16)
    upper = (row < col).astype(f32).astype(bf16)
    before = ((row // 8 == col // 8) & (col < row)).astype(f32).astype(bf16)
    inside = dot(hit16, upper)
    count = dot(hit16, jnp.ones((L, L), bf16))
    keys[...] = jnp.where(hit > 0.5, inside + dot(before, count.astype(bf16)), -1.0)

    share = itp[...]
    s_hi, rest = split(share)
    s_hi = s_hi.astype(f32)
    rest = share - s_hi
    s_mid = rest.astype(bf16).astype(f32)
    s_lo = rest - s_mid
    cell = key[...]
    fx = ((cell // NB) * 16 + sten[...]).astype(f32)
    seg = lax.rem(cell, NB).astype(f32)
    zero = jnp.zeros((3, L), f32)
    for bl in range(8):
        pick = [t[bl:bl + 1, :] for t in (s_hi, s_mid, s_lo, fx, seg)] + [zero]
        metaq[:, bl * L:(bl + 1) * L] = jnp.concatenate(pick, axis=0).astype(bf16)

    loads[4].wait()
    loads[5].wait()

    def cut(i, carry):
        rows = pl.ds(pl.multiple_of(i * L, L), L)
        w = wgt[rows, :]
        hi, lo = split(w)
        vals[rows, 0:L] = hi
        vals[rows, L:2 * L] = lo
        hi, lo = split(w * inn[rows, :])
        vals[rows, 2 * L:3 * L] = hi
        vals[rows, 3 * L:4 * L] = lo
        return carry

    lax.fori_loop(0, 8, cut, 0)

    for load in loads[6:]:
        load.wait()
    for j in range(2):
        tail = cc[j, 2, L - 8:L, :]
        cc[j, 2, L - 8:L, :] = jnp.where(iota((8, L), 0) < 7, tail, 0.0)
    lanes16 = iota((16, L), 1)
    for b in range(NB):
        tile = cyin[:, b * L:(b + 1) * L]
        if b == NB - 1:
            tile = jnp.where(lanes16 < L - 1, tile, 0.0)
        cyfield[0, b, 0] = tile

    def pack(field, out):
        def one(p, carry):
            out[p, :, 0] = field[:, 2 * p]
            out[p, :, 1] = field[:, 2 * p + 1]
            right = field[:, lax.rem(2 * p + 2, NB)]
            left = field[:, lax.rem(2 * p + NB - 1, NB)]
            out[p, :, 2] = jnp.where(iota(right.shape, right.ndim - 1) < 64, right, left)
            return carry

        lax.fori_loop(0, NPX, one, 0)

    def block(ext, k):
        return ext.at[:, :, :, pl.ds(pl.multiple_of(k * 16, 16), 16), :]

    def turn(send, ext, k, ssem, rsem):
        return pltpu.make_async_remote_copy(
            src_ref=send.at[ypeer(k)], dst_ref=block(ext, px),
            send_sem=ssem.at[k], recv_sem=rsem.at[k],
            device_id={"px": ypeer(k)}, device_id_type=MESH,
        )

    def turned(send, ext, k, ssem, rsem):
        source = lax.rem(px + NPX - k, NPX)
        return pltpu.make_async_remote_copy(
            src_ref=send.at[source], dst_ref=block(ext, source),
            send_sem=ssem.at[k], recv_sem=rsem.at[k],
            device_id={"px": ypeer(k)}, device_id_type=MESH,
        )

    def start_turn(send, ext, ssem, rsem):
        def one(k, carry):
            turn(send, ext, k, ssem, rsem).start()
            return carry

        lax.fori_loop(1, NPX, one, 0)
        ext[:, :, :, pl.ds(pl.multiple_of(px * 16, 16), 16), :] = send[px]

    def end_turn(send, ext, ssem, rsem):
        def one(k, carry):
            turned(send, ext, k, ssem, rsem).wait_recv()
            turn(send, ext, k, ssem, rsem).wait_send()
            return carry

        lax.fori_loop(1, NPX, one, 0)

    pack(cyfield, cysend)

    pl.semaphore_wait(barrier, NPX - 1 + NPY - 1)

    def edge(side):
        peer = ypeer(1 if side == 1 else NPX - 1)
        return pltpu.make_async_remote_copy(
            src_ref=cc.at[side], dst_ref=halo.at[side],
            send_sem=s_h.at[side], recv_sem=r_h.at[side],
            device_id={"px": peer}, device_id_type=MESH,
        )

    edge(0).start()
    edge(1).start()
    start_turn(cysend, cyx, s_c, r_c)

    def route(buf, land, k, ssem, rsem):
        return pltpu.make_async_remote_copy(
            src_ref=buf.at[k], dst_ref=land.at[k],
            send_sem=ssem.at[k], recv_sem=rsem.at[k],
            device_id={"py": opeer(k)}, device_id_type=MESH,
        )

    slot = iota((CAP, L), 0).astype(f32)

    def gather(k):
        base = pl.multiple_of(opeer(k) * 8, 8)
        mine = keys[pl.ds(base, 8), :]
        for bl in range(8):
            pbuf[:, bl * L:(bl + 1) * L] = (slot == mine[bl:bl + 1, :]).astype(f32).astype(bf16)
        meta = lax.dot_general(metaq[...], pbuf[...], NT, preferred_element_type=f32)
        out = dot(pbuf[...], vals[...])
        return meta, out[:, 0:L] + out[:, L:2 * L], out[:, 2 * L:3 * L] + out[:, 3 * L:4 * L]

    def send_rows(k, carry):
        meta, w, wd = gather(k)
        sm[k] = meta
        sw[k] = w
        sd[k] = wd
        route(sm, rm, k, s_m, r_m).start()
        route(sw, rw, k, s_w, r_w).start()
        return carry

    lax.fori_loop(1, NPY, send_rows, 0)

    meta, w, wd = gather(0)
    rm[0] = meta
    rw[0] = w
    rd[0] = wd

    for side in range(2):
        edge(side).wait_recv()
    lanes = iota((L, L), 1)
    for f in range(3):
        cc[2, f] = jnp.where(lanes < 64, halo[0, f], halo[1, f])
    end_turn(cysend, cyx, s_c, r_c)

    CH = 32

    def tiles(count, body):
        def one(j, carry):
            for f in range(2):
                body(j, f)
            return carry

        lax.fori_loop(0, count, one, 0)

    def chunks(body):
        def one(i, carry):
            rows = pl.ds(pl.multiple_of(i * CH, CH), CH)
            for f in range(2):
                body(f, rows)
            return carry

        lax.fori_loop(0, L // CH, one, 0)

    def bands_x(j, carry):
        for m, w in enumerate(band([cc[j, 2]], xshift)):
            wx[m, j] = w[0]
        return carry

    def bands_y(i, carry):
        rows = pl.ds(pl.multiple_of(i * 16, 16), 16)
        for m, w in enumerate(band([cyx[0, j, 0, rows, :] for j in range(3)], yshift)):
            for j in range(3):
                wy[m, j, rows, :] = w[j]
        return carry

    lax.fori_loop(0, 3, bands_x, 0)
    lax.fori_loop(0, 8, bands_y, 0)

    def sweep_x(v, j):
        return sweep(lambda m, _: wx[m, j], [v], xshift)[0]

    def sweep_y(v, rows, keep=3):
        return sweep(lambda m, j: wy[m, j, rows, :], v, yshift, keep)

    def first_x(j, f):
        ubuf[j, f] = sweep_x(cc[j, f], j)

    def first_y(f, rows):
        v = sweep_y([ubuf[j, f, rows, :] for j in range(3)], rows)
        for j in range(3):
            ubuf[j, f, rows, :] = v[j]

    tiles(3, first_x)
    chunks(first_y)

    def send_data(k, carry):
        route(sw, rw, k, s_w, r_w).wait_send()
        route(sd, rd, k, s_d, r_d).start()
        return carry

    lax.fori_loop(1, NPY, send_data, 0)

    pick = jnp.where(iota((8, L), 0) < 3, 1.0, 0.0).astype(bf16)
    target = iota((T, 4 * CAP), 0).astype(f32)

    def group(g, land, buf, ssem, rsem, with_meta, parts):
        for i in range(4):
            k = 4 * g + i

            @pl.when(k > 0)
            def _():
                if with_meta:
                    route(sm, rm, k, s_m, r_m).wait_recv()
                route(buf, land, k, ssem, rsem).wait_recv()

            meta = rm[k]
            s = lax.dot_general(meta.astype(bf16), pick, TN, preferred_element_type=f32)
            v = land[k]
            va = v * (1.0 - s)
            vs = v * s
            terms = (va * (1.0 - s), vs * s, vs * (1.0 - s)) if parts == 3 else (va, vs)
            rows = slice(i * CAP, (i + 1) * CAP)
            for n, term in enumerate(terms):
                hi, lo = split(term)
                rhs[rows, 2 * n * L:(2 * n + 1) * L] = hi
                rhs[rows, (2 * n + 1) * L:(2 * n + 2) * L] = lo
            tid[0:1, rows] = meta[4:5, :] * 32.0 + meta[3:4, :]
        onehot = (target == tid[0:1, :]).astype(f32).astype(bf16)
        width = 2 * parts * L
        part = dot(onehot, rhs[:, 0:width])

        @pl.when(g == 0)
        def _():
            acc[:, 0:width] = part

        @pl.when(g > 0)
        def _():
            acc[:, 0:width] += part

    def w_group(g, carry):
        group(g, rw, sw, s_w, r_w, True, 3)
        return carry

    lax.fori_loop(0, 4, w_group, 0)

    def column(n):
        return acc[:, 2 * n * L:(2 * n + 1) * L] + acc[:, (2 * n + 1) * L:(2 * n + 2) * L]

    tfield[0] = (column(0) + pltpu.roll(column(1), 1, 0)).reshape(NB, 2, 16, L)
    tfield[1] = column(2).reshape(NB, 2, 16, L)
    pack(tfield, tsend)
    start_turn(tsend, text, s_t, r_t)

    def d_group(g, carry):
        group(g, rd, sd, s_d, r_d, False, 2)
        return carry

    lax.fori_loop(0, 4, d_group, 0)
    bfield[0] = (column(0) + pltpu.roll(column(1), 1, 0)).reshape(NB, 2, 16, L)
    pack(bfield, bsend)
    start_turn(bsend, bext, s_b, r_b)
    end_turn(tsend, text, s_t, r_t)

    def spread(f, rows, keep=3):
        u = [ubuf[j, f, rows, :] for j in range(3)]
        return u, [tri(u[j], text[0, j, f, rows, :], text[1, j, f, rows, :]) for j in range(3)]

    def mid_chunk(f, rows):
        v = sweep_y(spread(f, rows)[1], rows)
        for j in range(3):
            gbuf[j, f, rows, :] = v[j]

    chunks(mid_chunk)

    def image_start(j, f):
        abuf[j, f] = cc[j, f] + sweep_x(gbuf[j, f], j)

    tiles(3, image_start)
    end_turn(bsend, bext, s_b, r_b)

    dots[...] = jnp.zeros_like(dots)

    def add_dot(n, a, b):
        dots[n] += jnp.sum((a * b).reshape(-1, 8, L), axis=0)

    def b_chunk(f, rows):
        v = sweep_y([bext[0, j, f, rows, :] for j in range(3)], rows)
        for j in range(3):
            gbuf[j, f, rows, :] = v[j]

    chunks(b_chunk)

    def residual_tile(j, f):
        r = sweep_x(gbuf[j, f], j) - abuf[j, f]
        rbuf[j, f] = r

        @pl.when(j < 2)
        def _():
            add_dot(0, r, r)

        ubuf[j, f] = sweep_x(r, j)

    tiles(3, residual_tile)

    def q_chunk(f, rows):
        u = sweep_y([ubuf[j, f, rows, :] for j in range(3)], rows)
        v = [tri(u[j], text[0, j, f, rows, :], text[1, j, f, rows, :]) for j in range(3)]
        for j in range(2):
            add_dot(1, u[j], v[j])
        v = sweep_y(v, rows)
        for j in range(3):
            gbuf[j, f, rows, :] = v[j]

    chunks(q_chunk)

    def q_tile(j, f):
        q = rbuf[j, f] + sweep_x(gbuf[j, f], j)
        qbuf[j, f] = q

        @pl.when(j < 2)
        def _():
            add_dot(2, q, q)

        ubuf[j, f] = sweep_x(q, j)

    tiles(3, q_tile)

    def p_up(f, rows):
        u = sweep_y([ubuf[j, f, rows, :] for j in range(3)], rows)
        v = [tri(u[j], text[0, j, f, rows, :], text[1, j, f, rows, :]) for j in range(3)]
        for j in range(2):
            add_dot(3, u[j], v[j])
        for j in range(3):
            ubuf[j, f, rows, :] = v[j]

    chunks(p_up)

    def p_down(f, rows):
        v = sweep_y([ubuf[j, f, rows, :] for j in range(3)], rows, 2)
        for j in range(2):
            gbuf[j, f, rows, :] = v[j]

    def p_tile(j, f):
        abuf[j, f] = qbuf[j, f] + sweep_x(gbuf[j, f], j)

    lines = [jnp.sum(dots[n], axis=0, keepdims=True) for n in range(4)]
    red1[0] = jnp.concatenate(lines + [jnp.zeros((4, L), f32)], axis=0)

    def sum1(k):
        return pltpu.make_async_remote_copy(
            src_ref=red1.at[0], dst_ref=red1.at[k], send_sem=s_1.at[k], recv_sem=r_1.at[k],
            device_id={"px": ypeer(k)}, device_id_type=MESH,
        )

    def sum2(k):
        return pltpu.make_async_remote_copy(
            src_ref=red2.at[0], dst_ref=red2.at[k], send_sem=s_2.at[k], recv_sem=r_2.at[k],
            device_id={"py": opeer(k)}, device_id_type=MESH,
        )

    for k in range(1, NPX):
        sum1(k).start()
    chunks(p_down)
    for k in range(1, NPX):
        sum1(k).wait_recv()
    total = red1[0]
    for k in range(1, NPX):
        total = total + red1[k]
    red2[0] = total
    for k in range(1, NPY):
        sum2(k).start()
    tiles(2, p_tile)
    for k in range(1, NPY):
        sum2(k).wait_recv()
    total = red2[0]
    for k in range(1, NPY):
        total = total + red2[k]
    sums = jnp.sum(total, axis=1, keepdims=True)
    rr, gain, qq, gain2 = [sums[n:n + 1, :] for n in range(4)]
    rq = rr + gain
    qp = qq + gain2
    alpha = rr / rq
    new = alpha * (alpha * qq) - rr
    beta = new / rr
    grow = 1.0 + beta
    alpha2 = new / (grow * grow * rq - 2.0 * alpha * grow * qq + alpha * alpha * qp)
    kr = alpha + alpha2 * grow
    kq = -alpha2 * alpha

    for j in range(2):
        for f in range(2):
            r = rbuf[j, f]
            q = qbuf[j, f]
            ctl[f, :, j * L:(j + 1) * L] = cc[j, f] + kr * r + kq * q
            res[f, :, j * L:(j + 1) * L] = r - kr * q - kq * abuf[j, f]

    for side in range(2):
        edge(side).wait_send()

    def drain_px(k, carry):
        sum1(k).wait_send()
        return carry

    def drain_py(k, carry):
        route(sm, rm, k, s_m, r_m).wait_send()
        route(sd, rd, k, s_d, r_d).wait_send()
        sum2(k).wait_send()
        return carry

    lax.fori_loop(1, NPX, drain_px, 0)
    lax.fori_loop(1, NPY, drain_py, 0)


def shards(control_start, coef_x, coef_y, innovation, obs_weight, interp, obs_owner, cell_key, stencil):
    dma = pltpu.SemaphoreType.DMA
    vm = pltpu.VMEM
    field = vm((3, 2, L, L), f32)
    scratch = [
        vm((8, L), jnp.int32), vm((8, L), jnp.int32), vm((8, L), jnp.int32), vm((8, L), f32),
        vm((ROWS, L), f32), vm((ROWS, L), f32), vm((16, NB * L), f32), dma((11,)),
        vm((2 * M + 1, 3, L, L), f32), vm((2 * M + 1, 3, L, L), f32),
        vm((L, L), f32), vm((ROWS, 4 * L), bf16), vm((8, ROWS), bf16), vm((CAP, ROWS), bf16),
        vm((NPY, CAP, L), f32), vm((NPY, CAP, L), f32), vm((NPY, 8, CAP), f32),
        vm((NPY, CAP, L), f32), vm((NPY, CAP, L), f32), vm((NPY, 8, CAP), f32),
        vm((4 * CAP, 6 * L), bf16), vm((8, 4 * CAP), f32), vm((T, 6 * L), f32),
        vm((2, NB, 2, 16, L), f32), vm((NPX, 2, 3, 2, 16, L), f32),
        vm((1, NB, 2, 16, L), f32), vm((NPX, 1, 3, 2, 16, L), f32),
        vm((1, NB, 1, 16, L), f32), vm((NPX, 1, 3, 1, 16, L), f32),
        vm((3, 3, L, L), f32), vm((2, 3, L, L), f32),
        vm((2, 3, 2, L, L), f32), vm((1, 3, 2, L, L), f32), vm((1, 3, 1, L, L), f32),
        field, field, field, field, field,
        vm((4, 8, L), f32), vm((NPX, 8, L), f32), vm((NPY, 8, L), f32),
        dma((NPY,)), dma((NPY,)), dma((NPY,)), dma((NPY,)), dma((NPY,)), dma((NPY,)),
        dma((NPX,)), dma((NPX,)), dma((NPX,)), dma((NPX,)), dma((NPX,)), dma((NPX,)),
        dma((2,)), dma((2,)), dma((NPX,)), dma((NPX,)), dma((NPY,)), dma((NPY,)),
    ]
    out = jax.ShapeDtypeStruct((2, L, 2 * L), f32)
    control, residual = pl.pallas_call(
        kernel,
        out_shape=(out, out),
        in_specs=[pl.BlockSpec(memory_space=pltpu.HBM)] * 9,
        out_specs=(pl.BlockSpec(memory_space=pltpu.VMEM),) * 2,
        scratch_shapes=scratch,
        compiler_params=pltpu.CompilerParams(
            collective_id=0, has_side_effects=True, vmem_limit_bytes=60 * 1024 * 1024
        ),
        name="assimilate",
    )(
        obs_owner.reshape(8, L), cell_key.reshape(8, L), stencil.reshape(8, L), interp.reshape(8, L),
        innovation, obs_weight, control_start.reshape(2, L, 2 * L), coef_x.reshape(L, 2 * L),
        coef_y.reshape(16, NB * L),
    )
    shape = control_start.shape
    return control.reshape(shape), residual.reshape(shape)


def solution(mesh):
    return jax.shard_map(
        shards,
        mesh=mesh,
        in_specs=(
            P(None, "py", None, "px"),
            P("py", None, "px"),
            P("py", "px", None),
            P(("px", "py"), None),
            P(("px", "py"), None),
            P(("px", "py")),
            P(("px", "py"), None),
            P(("px", "py")),
            P(("px", "py")),
        ),
        out_specs=(P(None, "py", None, "px"), P(None, "py", None, "px")),
        check_vma=False,
    )
```

```python
import jax
import jax.numpy as jnp
from jax import lax
from jax.experimental import pallas as pl
from jax.experimental.pallas import tpu as pltpu
from jax.sharding import PartitionSpec as P

NPX = 8
NPY = 16
CAP = 192
ROWS = 1024
L = 128
M = 4
NB = 16
T = 512
f32 = jnp.float32
bf16 = jnp.bfloat16
MESH = pl.DeviceIdType.MESH
NT = (((1,), (1,)), ((), ()))
TN = (((0,), (0,)), ((), ()))


def dot(a, b):
    return jnp.dot(a, b, preferred_element_type=f32)


def iota(shape, axis):
    return lax.broadcasted_iota(jnp.int32, shape, axis)


def split(v):
    hi = v.astype(bf16)
    return hi, (v - hi.astype(f32)).astype(bf16)


def xshift(v, k):
    return [pltpu.roll(t, (-k) % L, 0) for t in v] if k else v


def yshift(v, k):
    if k == 0:
        return v
    lane = iota(v[0].shape, 1)
    r = [pltpu.roll(t, (-k) % L, 1) for t in v]
    n = len(v)
    if k > 0:
        return [jnp.where(lane < L - k, r[j], r[(j + 1) % n]) for j in range(n)]
    return [jnp.where(lane >= -k, r[j], r[(j + n - 1) % n]) for j in range(n)]


def mul(a, b):
    return [x * y for x, y in zip(a, b)]


def add(*terms):
    total = terms[0]
    for t in terms[1:]:
        total = [x + y for x, y in zip(total, t)]
    return total


def band(c, shift):
    a = shift(c, -1)
    d = [1.0 - x - y for x, y in zip(c, a)]
    p0 = add(mul(d, d), mul(c, c), mul(a, a))
    p1 = mul(c, add(d, shift(d, 1)))
    p2 = mul(c, shift(c, 1))
    n1, n2 = shift(p1, -1), shift(p2, -2)
    up1 = shift(p1, 1)
    b0 = add(mul(p0, p0), mul(p1, p1), mul(p2, p2), mul(n1, n1), mul(n2, n2))
    b1 = add(mul(p1, add(p0, shift(p0, 1))), mul(p2, up1), mul(n1, shift(p2, -1)))
    b2 = add(mul(p0, p2), mul(p1, up1), mul(p2, shift(p0, 2)))
    b3 = add(mul(p1, shift(p2, 1)), mul(p2, shift(p1, 2)))
    b4 = mul(p2, shift(p2, 2))
    return [shift(b4, -4), shift(b3, -3), shift(b2, -2), shift(b1, -1), b0, b1, b2, b3, b4]


def sweep(w, v, shift, keep=3):
    total = None
    for m in range(2 * M + 1):
        moved = shift(v, m - M)[:keep]
        term = [w(m, j) * t for j, t in enumerate(moved)]
        total = term if total is None else add(total, term)
    return total


def tri(u, d, e):
    eu = e * u
    return d * u + e * pltpu.roll(u, u.shape[0] - 1, 0) + pltpu.roll(eu, 1, 0)


def kernel(
    h_own, h_key, h_sten, h_itp, h_inn, h_wgt, h_c, h_cx, h_cy, ctl, res,
    own, key, sten, itp, inn, wgt, cyin, s_in, wx, wy,
    keys, vals, metaq, pbuf, sw, sd, sm, rw, rd, rm, rhs, tid, acc,
    tfield, tsend, bfield, bsend, cyfield, cysend, cc, halo, text, bext, cyx,
    ubuf, gbuf, abuf, rbuf, qbuf, dots, red1, red2, onehot, shares_of,
    s_m, s_w, s_d, r_m, r_w, r_d, s_t, r_t, s_b, r_b, s_c, r_c, s_h, r_h, s_1, r_1, s_2, r_2,
):
    px = lax.axis_index("px")
    py = lax.axis_index("py")

    def ypeer(k):
        return lax.rem(px + k, NPX)

    def opeer(k):
        k = lax.rem(k + lax.rem(px, 2) * (2 * NPY - 2 * k), NPY)
        x = lax.rem(py // 4 + lax.rem(k, 4), 4)
        z = lax.rem(lax.rem(py, 4) + k // 4 + 4 - lax.rem(k, 4), 4)
        return x * 4 + z

    loads = [(h_own, own), (h_key, key), (h_sten, sten), (h_itp, itp), (h_wgt, wgt), (h_inn, inn), (h_cy, cyin)]
    for j in range(2):
        lanes = slice(j * L, (j + 1) * L)
        loads.append((h_c.at[:, :, lanes], cc.at[j, 0:2]))
        loads.append((h_cx.at[:, lanes], cc.at[j, 2]))
    loads = [pltpu.make_async_copy(a, b, s_in.at[n]) for n, (a, b) in enumerate(loads)]
    for load in loads:
        load.start()

    barrier = pltpu.get_barrier_semaphore()

    def greet_px(k, carry):
        pl.semaphore_signal(barrier, inc=1, device_id={"px": ypeer(k)}, device_id_type=MESH)
        return carry

    def greet_py(k, carry):
        pl.semaphore_signal(barrier, inc=1, device_id={"py": opeer(k)}, device_id_type=MESH)
        return carry

    for k in range(1, NPX):
        greet_px(k, 0)
    for k in range(1, NPY):
        greet_py(k, 0)

    for n in range(4):
        loads[n].wait()
    row = iota((L, L), 0)
    col = iota((L, L), 1)
    owner = own[...]
    hit = jnp.concatenate([(owner == d).astype(f32) for d in range(NPY)], axis=0)
    hit16 = hit.astype(bf16)
    upper = (row < col).astype(f32).astype(bf16)
    before = ((row // 8 == col // 8) & (col < row)).astype(f32).astype(bf16)
    inside = dot(hit16, upper)
    count = dot(hit16, jnp.ones((L, L), bf16))
    keys[...] = jnp.where(hit > 0.5, inside + dot(before, count.astype(bf16)), -1.0)

    share = itp[...]
    s_hi, rest = split(share)
    s_hi = s_hi.astype(f32)
    rest = share - s_hi
    s_mid = rest.astype(bf16).astype(f32)
    s_lo = rest - s_mid
    cell = key[...]
    fx = ((cell // NB) * 16 + sten[...]).astype(f32)
    seg = lax.rem(cell, NB).astype(f32)
    zero = jnp.zeros((3, L), f32)
    for bl in range(8):
        pick = [t[bl:bl + 1, :] for t in (s_hi, s_mid, s_lo, fx, seg)] + [zero]
        metaq[:, bl * L:(bl + 1) * L] = jnp.concatenate(pick, axis=0).astype(bf16)

    loads[4].wait()
    loads[5].wait()

    def cut(i, carry):
        rows = pl.ds(pl.multiple_of(i * L, L), L)
        w = wgt[rows, :]
        hi, lo = split(w)
        vals[rows, 0:L] = hi
        vals[rows, L:2 * L] = lo
        hi, lo = split(w * inn[rows, :])
        vals[rows, 2 * L:3 * L] = hi
        vals[rows, 3 * L:4 * L] = lo
        return carry

    lax.fori_loop(0, 8, cut, 0)

    def pack(field, out):
        def one(p, carry):
            out[p, :, 0] = field[:, 2 * p]
            out[p, :, 1] = field[:, 2 * p + 1]
            right = field[:, lax.rem(2 * p + 2, NB)]
            left = field[:, lax.rem(2 * p + NB - 1, NB)]
            out[p, :, 2] = jnp.where(iota(right.shape, right.ndim - 1) < 64, right, left)
            return carry

        lax.fori_loop(0, NPX, one, 0)

    def block(ext, k):
        return ext.at[:, :, :, pl.ds(pl.multiple_of(k * 16, 16), 16), :]

    def turn(send, ext, k, ssem, rsem):
        return pltpu.make_async_remote_copy(
            src_ref=send.at[ypeer(k)], dst_ref=block(ext, px),
            send_sem=ssem.at[k], recv_sem=rsem.at[k],
            device_id={"px": ypeer(k)}, device_id_type=MESH,
        )

    def turned(send, ext, k, ssem, rsem):
        source = lax.rem(px + NPX - k, NPX)
        return pltpu.make_async_remote_copy(
            src_ref=send.at[source], dst_ref=block(ext, source),
            send_sem=ssem.at[k], recv_sem=rsem.at[k],
            device_id={"px": ypeer(k)}, device_id_type=MESH,
        )

    def start_turn(send, ext, ssem, rsem):
        def one(k, carry):
            turn(send, ext, k, ssem, rsem).start()
            return carry

        lax.fori_loop(1, NPX, one, 0)
        ext[:, :, :, pl.ds(pl.multiple_of(px * 16, 16), 16), :] = send[px]

    def end_turn(send, ext, ssem, rsem):
        def one(k, carry):
            turned(send, ext, k, ssem, rsem).wait_recv()
            return carry

        lax.fori_loop(1, NPX, one, 0)

    pl.semaphore_wait(barrier, NPX - 1 + NPY - 1)

    def edge(side):
        peer = ypeer(1 if side == 1 else NPX - 1)
        return pltpu.make_async_remote_copy(
            src_ref=cc.at[side], dst_ref=halo.at[side],
            send_sem=s_h.at[side], recv_sem=r_h.at[side],
            device_id={"px": peer}, device_id_type=MESH,
        )

    def route(buf, land, k, ssem, rsem):
        return pltpu.make_async_remote_copy(
            src_ref=buf.at[k], dst_ref=land.at[k],
            send_sem=ssem.at[k], recv_sem=rsem.at[k],
            device_id={"py": opeer(k)}, device_id_type=MESH,
        )

    slot = iota((CAP, L), 0).astype(f32)

    def gather(k):
        base = pl.multiple_of(opeer(k) * 8, 8)
        mine = keys[pl.ds(base, 8), :]
        for bl in range(8):
            pbuf[:, bl * L:(bl + 1) * L] = (slot == mine[bl:bl + 1, :]).astype(f32).astype(bf16)
        meta = lax.dot_general(metaq[...], pbuf[...], NT, preferred_element_type=f32)
        out = dot(pbuf[...], vals[...])
        return meta, out[:, 0:L] + out[:, L:2 * L], out[:, 2 * L:3 * L] + out[:, 3 * L:4 * L]

    def send_rows(k, carry):
        meta, w, wd = gather(k)
        sm[k] = meta
        sw[k] = w
        sd[k] = wd
        route(sm, rm, k, s_m, r_m).start()
        route(sw, rw, k, s_w, r_w).start()
        return carry

    lax.fori_loop(1, NPY, send_rows, 0)

    meta, w, wd = gather(0)
    rm[0] = meta
    rw[0] = w
    rd[0] = wd

    for load in loads[6:]:
        load.wait()
    for j in range(2):
        tail = cc[j, 2, L - 8:L, :]
        cc[j, 2, L - 8:L, :] = jnp.where(iota((8, L), 0) < 7, tail, 0.0)
    lanes16 = iota((16, L), 1)
    for b in range(NB):
        tile = cyin[:, b * L:(b + 1) * L]
        if b == NB - 1:
            tile = jnp.where(lanes16 < L - 1, tile, 0.0)
        cyfield[0, b, 0] = tile

    def free_turn(send, ext, ssem, rsem):
        def one(k, carry):
            turn(send, ext, k, ssem, rsem).wait_send()
            return carry

        lax.fori_loop(1, NPX, one, 0)

    pack(cyfield, cysend)

    edge(0).start()
    edge(1).start()
    start_turn(cysend, cyx, s_c, r_c)

    for side in range(2):
        edge(side).wait_recv()
    lanes = iota((L, L), 1)
    for f in range(3):
        cc[2, f] = jnp.where(lanes < 64, halo[0, f], halo[1, f])
    end_turn(cysend, cyx, s_c, r_c)

    CH = 64

    def tiles(count, body):
        def one(j, carry):
            for f in range(2):
                body(j, f)
            return carry

        lax.fori_loop(0, count, one, 0)

    def chunks(body):
        def one(i, carry):
            rows = pl.ds(pl.multiple_of(i * CH, CH), CH)
            for f in range(2):
                body(f, rows)
            return carry

        lax.fori_loop(0, L // CH, one, 0)

    def bands_x(j, carry):
        for m, w in enumerate(band([cc[j, 2]], xshift)):
            wx[m, j] = w[0]
        return carry

    def bands_y(i, carry):
        rows = pl.ds(pl.multiple_of(i * 16, 16), 16)
        for m, w in enumerate(band([cyx[0, j, 0, rows, :] for j in range(3)], yshift)):
            for j in range(3):
                wy[m, j, rows, :] = w[j]
        return carry

    lax.fori_loop(0, 3, bands_x, 0)
    lax.fori_loop(0, 8, bands_y, 0)

    def sweep_x(v, j):
        return sweep(lambda m, _: wx[m, j], [v], xshift)[0]

    def sweep_y(v, rows, keep=3):
        return sweep(lambda m, j: wy[m, j, rows, :], v, yshift, keep)

    def first_x(j, f):
        ubuf[j, f] = sweep_x(cc[j, f], j)

    def first_y(f, rows):
        v = sweep_y([ubuf[j, f, rows, :] for j in range(3)], rows)
        for j in range(3):
            ubuf[j, f, rows, :] = v[j]

    tiles(3, first_x)
    chunks(first_y)

    def send_data(k, carry):
        route(sm, rm, k, s_m, r_m).wait_send()
        route(sw, rw, k, s_w, r_w).wait_send()
        route(sd, rd, k, s_d, r_d).start()
        return carry

    lax.fori_loop(1, NPY, send_data, 0)

    pick = jnp.where(iota((8, L), 0) < 3, 1.0, 0.0).astype(bf16)
    target = iota((T, 4 * CAP), 0).astype(f32)

    def group(g, land, buf, ssem, rsem, with_meta, parts):
        for i in range(4):
            k = 4 * g + i

            @pl.when(k > 0)
            def _():
                if with_meta:
                    route(sm, rm, k, s_m, r_m).wait_recv()
                route(buf, land, k, ssem, rsem).wait_recv()

            rows = slice(i * CAP, (i + 1) * CAP)
            if with_meta:
                meta = rm[k]
                s = lax.dot_general(meta.astype(bf16), pick, TN, preferred_element_type=f32)
                shares_of[k] = s
                tid[0:1, rows] = meta[4:5, :] * 32.0 + meta[3:4, :]
            else:
                s = shares_of[k]
            v = land[k]
            va = v * (1.0 - s)
            vs = v * s
            terms = (va * (1.0 - s), vs * s, vs * (1.0 - s)) if parts == 3 else (va, vs)
            for n, term in enumerate(terms):
                hi, lo = split(term)
                rhs[rows, 2 * n * L:(2 * n + 1) * L] = hi
                rhs[rows, (2 * n + 1) * L:(2 * n + 2) * L] = lo
        if with_meta:
            onehot[g] = (target == tid[0:1, :]).astype(f32).astype(bf16)
        width = 2 * parts * L
        part = dot(onehot[g], rhs[:, 0:width])

        @pl.when(g == 0)
        def _():
            acc[:, 0:width] = part

        @pl.when(g > 0)
        def _():
            acc[:, 0:width] += part

    def w_group(g, carry):
        group(g, rw, sw, s_w, r_w, True, 3)
        return carry

    lax.fori_loop(0, 4, w_group, 0)

    def column(n):
        return acc[:, 2 * n * L:(2 * n + 1) * L] + acc[:, (2 * n + 1) * L:(2 * n + 2) * L]

    tfield[0] = (column(0) + pltpu.roll(column(1), 1, 0)).reshape(NB, 2, 16, L)
    tfield[1] = column(2).reshape(NB, 2, 16, L)
    pack(tfield, tsend)
    start_turn(tsend, text, s_t, r_t)

    def d_group(g, carry):
        group(g, rd, sd, s_d, r_d, False, 2)
        return carry

    lax.fori_loop(0, 4, d_group, 0)
    bfield[0] = (column(0) + pltpu.roll(column(1), 1, 0)).reshape(NB, 2, 16, L)
    pack(bfield, bsend)
    start_turn(bsend, bext, s_b, r_b)

    def drain_py(k, carry):
        route(sd, rd, k, s_d, r_d).wait_send()
        return carry

    for side in range(2):
        edge(side).wait_send()
    free_turn(cysend, cyx, s_c, r_c)
    end_turn(tsend, text, s_t, r_t)

    def spread(f, rows, keep=3):
        u = [ubuf[j, f, rows, :] for j in range(3)]
        return u, [tri(u[j], text[0, j, f, rows, :], text[1, j, f, rows, :]) for j in range(3)]

    def mid_chunk(f, rows):
        v = sweep_y(spread(f, rows)[1], rows)
        for j in range(3):
            gbuf[j, f, rows, :] = v[j]

    chunks(mid_chunk)

    def image_start(j, f):
        abuf[j, f] = cc[j, f] + sweep_x(gbuf[j, f], j)

    tiles(3, image_start)
    lax.fori_loop(1, NPY, drain_py, 0)
    free_turn(tsend, text, s_t, r_t)
    end_turn(bsend, bext, s_b, r_b)

    dots[...] = jnp.zeros_like(dots)

    def add_dot(n, a, b):
        dots[n] += jnp.sum((a * b).reshape(-1, 8, L), axis=0)

    def b_chunk(f, rows):
        v = sweep_y([bext[0, j, f, rows, :] for j in range(3)], rows)
        for j in range(3):
            gbuf[j, f, rows, :] = v[j]

    chunks(b_chunk)

    def residual_tile(j, f):
        r = sweep_x(gbuf[j, f], j) - abuf[j, f]
        rbuf[j, f] = r

        @pl.when(j < 2)
        def _():
            add_dot(0, r, r)

        ubuf[j, f] = sweep_x(r, j)

    tiles(3, residual_tile)

    def q_chunk(f, rows):
        u = sweep_y([ubuf[j, f, rows, :] for j in range(3)], rows)
        v = [tri(u[j], text[0, j, f, rows, :], text[1, j, f, rows, :]) for j in range(3)]
        for j in range(2):
            add_dot(1, u[j], v[j])
        v = sweep_y(v, rows)
        for j in range(3):
            gbuf[j, f, rows, :] = v[j]

    chunks(q_chunk)

    def q_tile(j, f):
        q = rbuf[j, f] + sweep_x(gbuf[j, f], j)
        qbuf[j, f] = q

        @pl.when(j < 2)
        def _():
            add_dot(2, q, q)

        ubuf[j, f] = sweep_x(q, j)

    tiles(3, q_tile)

    def p_up(f, rows):
        u = sweep_y([ubuf[j, f, rows, :] for j in range(3)], rows)
        v = [tri(u[j], text[0, j, f, rows, :], text[1, j, f, rows, :]) for j in range(3)]
        for j in range(2):
            add_dot(3, u[j], v[j])
        for j in range(3):
            ubuf[j, f, rows, :] = v[j]

    chunks(p_up)

    def p_down(f, rows):
        v = sweep_y([ubuf[j, f, rows, :] for j in range(3)], rows, 2)
        for j in range(2):
            gbuf[j, f, rows, :] = v[j]

    def p_tile(j, f):
        abuf[j, f] = qbuf[j, f] + sweep_x(gbuf[j, f], j)

    lines = [jnp.sum(dots[n], axis=0, keepdims=True) for n in range(4)]
    red1[0] = jnp.concatenate(lines + [jnp.zeros((4, L), f32)], axis=0)

    def sum1(k):
        return pltpu.make_async_remote_copy(
            src_ref=red1.at[0], dst_ref=red1.at[k], send_sem=s_1.at[k], recv_sem=r_1.at[k],
            device_id={"px": ypeer(k)}, device_id_type=MESH,
        )

    def sum2(k):
        return pltpu.make_async_remote_copy(
            src_ref=red2.at[0], dst_ref=red2.at[k], send_sem=s_2.at[k], recv_sem=r_2.at[k],
            device_id={"py": opeer(k)}, device_id_type=MESH,
        )

    def merge(count, send, buf):
        for k in range(1, count):
            send(k).wait_recv()
        total = buf[0]
        for k in range(1, count):
            total = total + buf[k]
        return total

    for k in range(1, NPX):
        sum1(k).start()
    chunks(p_down)
    free_turn(bsend, bext, s_b, r_b)
    red2[0] = merge(NPX, sum1, red1)
    for k in range(1, NPY):
        sum2(k).start()
    for k in range(1, NPX):
        sum1(k).wait_send()
    tiles(2, p_tile)
    total = merge(NPY, sum2, red2)
    sums = jnp.sum(total, axis=1, keepdims=True)
    rr, gain, qq, gain2 = [sums[n:n + 1, :] for n in range(4)]
    rq = rr + gain
    qp = qq + gain2
    alpha = rr / rq
    new = alpha * (alpha * qq) - rr
    beta = new / rr
    grow = 1.0 + beta
    alpha2 = new / (grow * grow * rq - 2.0 * alpha * grow * qq + alpha * alpha * qp)
    kr = alpha + alpha2 * grow
    kq = -alpha2 * alpha

    for j in range(2):
        for f in range(2):
            r = rbuf[j, f]
            q = qbuf[j, f]
            ctl[f, :, j * L:(j + 1) * L] = cc[j, f] + kr * r + kq * q
            res[f, :, j * L:(j + 1) * L] = r - kr * q - kq * abuf[j, f]

    for k in range(1, NPY):
        sum2(k).wait_send()


def shards(control_start, coef_x, coef_y, innovation, obs_weight, interp, obs_owner, cell_key, stencil):
    dma = pltpu.SemaphoreType.DMA
    vm = pltpu.VMEM
    field = vm((3, 2, L, L), f32)
    scratch = [
        vm((8, L), jnp.int32), vm((8, L), jnp.int32), vm((8, L), jnp.int32), vm((8, L), f32),
        vm((ROWS, L), f32), vm((ROWS, L), f32), vm((16, NB * L), f32), dma((11,)),
        vm((2 * M + 1, 3, L, L), f32), vm((2 * M + 1, 3, L, L), f32),
        vm((L, L), f32), vm((ROWS, 4 * L), bf16), vm((8, ROWS), bf16), vm((CAP, ROWS), bf16),
        vm((NPY, CAP, L), f32), vm((NPY, CAP, L), f32), vm((NPY, 8, CAP), f32),
        vm((NPY, CAP, L), f32), vm((NPY, CAP, L), f32), vm((NPY, 8, CAP), f32),
        vm((4 * CAP, 6 * L), bf16), vm((8, 4 * CAP), f32), vm((T, 6 * L), f32),
        vm((2, NB, 2, 16, L), f32), vm((NPX, 2, 3, 2, 16, L), f32),
        vm((1, NB, 2, 16, L), f32), vm((NPX, 1, 3, 2, 16, L), f32),
        vm((1, NB, 1, 16, L), f32), vm((NPX, 1, 3, 1, 16, L), f32),
        vm((3, 3, L, L), f32), vm((2, 3, L, L), f32),
        vm((2, 3, 2, L, L), f32), vm((1, 3, 2, L, L), f32), vm((1, 3, 1, L, L), f32),
        field, field, field, field, field,
        vm((4, 8, L), f32), vm((NPX, 8, L), f32), vm((NPY, 8, L), f32),
        vm((4, T, 4 * CAP), bf16), vm((NPY, CAP, L), f32),
        dma((NPY,)), dma((NPY,)), dma((NPY,)), dma((NPY,)), dma((NPY,)), dma((NPY,)),
        dma((NPX,)), dma((NPX,)), dma((NPX,)), dma((NPX,)), dma((NPX,)), dma((NPX,)),
        dma((2,)), dma((2,)), dma((NPX,)), dma((NPX,)), dma((NPY,)), dma((NPY,)),
    ]
    out = jax.ShapeDtypeStruct((2, L, 2 * L), f32)
    control, residual = pl.pallas_call(
        kernel,
        out_shape=(out, out),
        in_specs=[pl.BlockSpec(memory_space=pltpu.HBM)] * 9,
        out_specs=(pl.BlockSpec(memory_space=pltpu.VMEM),) * 2,
        scratch_shapes=scratch,
        compiler_params=pltpu.CompilerParams(
            collective_id=0, has_side_effects=True, vmem_limit_bytes=60 * 1024 * 1024
        ),
        name="assimilate",
    )(
        obs_owner.reshape(8, L), cell_key.reshape(8, L), stencil.reshape(8, L), interp.reshape(8, L),
        innovation, obs_weight, control_start.reshape(2, L, 2 * L), coef_x.reshape(L, 2 * L),
        coef_y.reshape(16, NB * L),
    )
    shape = control_start.shape
    return control.reshape(shape), residual.reshape(shape)


def solution(mesh):
    return jax.shard_map(
        shards,
        mesh=mesh,
        in_specs=(
            P(None, "py", None, "px"),
            P("py", None, "px"),
            P("py", "px", None),
            P(("px", "py"), None),
            P(("px", "py"), None),
            P(("px", "py")),
            P(("px", "py"), None),
            P(("px", "py")),
            P(("px", "py")),
        ),
        out_specs=(P(None, "py", None, "px"), P(None, "py", None, "px")),
        check_vma=False,
    )
```

```python
import jax
import jax.numpy as jnp
from jax import lax
from jax.experimental import pallas as pl
from jax.experimental.pallas import tpu as pltpu
from jax.sharding import PartitionSpec as P

NPX = 8
NPY = 16
CAP = 192
ROWS = 1024
L = 128
M = 4
NB = 16
T = 512
f32 = jnp.float32
bf16 = jnp.bfloat16
MESH = pl.DeviceIdType.MESH
NT = (((1,), (1,)), ((), ()))
TN = (((0,), (0,)), ((), ()))


def dot(a, b):
    return jnp.dot(a, b, preferred_element_type=f32)


def iota(shape, axis):
    return lax.broadcasted_iota(jnp.int32, shape, axis)


def split(v):
    hi = v.astype(bf16)
    return hi, (v - hi.astype(f32)).astype(bf16)


def xshift(v, k):
    return [pltpu.roll(t, (-k) % L, 0) for t in v] if k else v


def yshift(v, k):
    if k == 0:
        return v
    lane = iota(v[0].shape, 1)
    r = [pltpu.roll(t, (-k) % L, 1) for t in v]
    n = len(v)
    if k > 0:
        return [jnp.where(lane < L - k, r[j], r[(j + 1) % n]) for j in range(n)]
    return [jnp.where(lane >= -k, r[j], r[(j + n - 1) % n]) for j in range(n)]


def mul(a, b):
    return [x * y for x, y in zip(a, b)]


def add(*terms):
    total = terms[0]
    for t in terms[1:]:
        total = [x + y for x, y in zip(total, t)]
    return total


def band(c, shift):
    a = shift(c, -1)
    d = [1.0 - x - y for x, y in zip(c, a)]
    p0 = add(mul(d, d), mul(c, c), mul(a, a))
    p1 = mul(c, add(d, shift(d, 1)))
    p2 = mul(c, shift(c, 1))
    n1, n2 = shift(p1, -1), shift(p2, -2)
    up1 = shift(p1, 1)
    b0 = add(mul(p0, p0), mul(p1, p1), mul(p2, p2), mul(n1, n1), mul(n2, n2))
    b1 = add(mul(p1, add(p0, shift(p0, 1))), mul(p2, up1), mul(n1, shift(p2, -1)))
    b2 = add(mul(p0, p2), mul(p1, up1), mul(p2, shift(p0, 2)))
    b3 = add(mul(p1, shift(p2, 1)), mul(p2, shift(p1, 2)))
    b4 = mul(p2, shift(p2, 2))
    return [shift(b4, -4), shift(b3, -3), shift(b2, -2), shift(b1, -1), b0, b1, b2, b3, b4]


def sweep(w, v, shift, keep=3):
    total = None
    for m in range(2 * M + 1):
        moved = shift(v, m - M)[:keep]
        term = [w(m, j) * t for j, t in enumerate(moved)]
        total = term if total is None else add(total, term)
    return total


def tri(u, d, e):
    eu = e * u
    return d * u + e * pltpu.roll(u, u.shape[0] - 1, 0) + pltpu.roll(eu, 1, 0)


def kernel(
    h_own, h_key, h_sten, h_itp, h_inn, h_wgt, h_c, h_cx, h_cy, o_r, o_q, o_p, o_k,
    own, key, sten, itp, inn, wgt, cyin, s_in, wx, wy,
    keys, vals, metaq, pbuf, sw, sd, sm, rw, rd, rm, rhs, tid, acc,
    tfield, tsend, bfield, bsend, cyfield, cysend, cc, halo, text, bext, cyx,
    ubuf, gbuf, abuf, rbuf, qbuf, dots, red1, red2, onehot, shares_of,
    s_m, s_w, s_d, r_m, r_w, r_d, s_t, r_t, s_b, r_b, s_c, r_c, s_h, r_h, s_1, r_1, s_2, r_2, s_o,
):
    px = lax.axis_index("px")
    py = lax.axis_index("py")

    def ypeer(k):
        return lax.rem(px + k, NPX)

    def opeer(k):
        k = lax.rem(k + lax.rem(px, 2) * (2 * NPY - 2 * k), NPY)
        x = lax.rem(py // 4 + lax.rem(k, 4), 4)
        z = lax.rem(lax.rem(py, 4) + k // 4 + 4 - lax.rem(k, 4), 4)
        return x * 4 + z

    loads = [(h_own, own), (h_key, key), (h_sten, sten), (h_itp, itp), (h_wgt, wgt), (h_inn, inn), (h_cy, cyin)]
    for j in range(2):
        lanes = slice(j * L, (j + 1) * L)
        loads.append((h_c.at[:, :, lanes], cc.at[j, 0:2]))
        loads.append((h_cx.at[:, lanes], cc.at[j, 2]))
    loads = [pltpu.make_async_copy(a, b, s_in.at[n]) for n, (a, b) in enumerate(loads)]
    for load in loads:
        load.start()

    barrier = pltpu.get_barrier_semaphore()

    def greet_px(k, carry):
        pl.semaphore_signal(barrier, inc=1, device_id={"px": ypeer(k)}, device_id_type=MESH)
        return carry

    def greet_py(k, carry):
        pl.semaphore_signal(barrier, inc=1, device_id={"py": opeer(k)}, device_id_type=MESH)
        return carry

    for k in range(1, NPX):
        greet_px(k, 0)
    for k in range(1, NPY):
        greet_py(k, 0)

    for n in range(4):
        loads[n].wait()
    row = iota((L, L), 0)
    col = iota((L, L), 1)
    owner = own[...]
    hit = jnp.concatenate([(owner == d).astype(f32) for d in range(NPY)], axis=0)
    hit16 = hit.astype(bf16)
    upper = (row < col).astype(f32).astype(bf16)
    before = ((row // 8 == col // 8) & (col < row)).astype(f32).astype(bf16)
    inside = dot(hit16, upper)
    count = dot(hit16, jnp.ones((L, L), bf16))
    keys[...] = jnp.where(hit > 0.5, inside + dot(before, count.astype(bf16)), -1.0)

    share = itp[...]
    s_hi, rest = split(share)
    s_hi = s_hi.astype(f32)
    rest = share - s_hi
    s_mid = rest.astype(bf16).astype(f32)
    s_lo = rest - s_mid
    cell = key[...]
    fx = ((cell // NB) * 16 + sten[...]).astype(f32)
    seg = lax.rem(cell, NB).astype(f32)
    zero = jnp.zeros((3, L), f32)
    for bl in range(8):
        pick = [t[bl:bl + 1, :] for t in (s_hi, s_mid, s_lo, fx, seg)] + [zero]
        metaq[:, bl * L:(bl + 1) * L] = jnp.concatenate(pick, axis=0).astype(bf16)

    loads[4].wait()
    loads[5].wait()

    def cut(i, carry):
        rows = pl.ds(pl.multiple_of(i * L, L), L)
        w = wgt[rows, :]
        hi, lo = split(w)
        vals[rows, 0:L] = hi
        vals[rows, L:2 * L] = lo
        hi, lo = split(w * inn[rows, :])
        vals[rows, 2 * L:3 * L] = hi
        vals[rows, 3 * L:4 * L] = lo
        return carry

    lax.fori_loop(0, 8, cut, 0)

    def pack(field, out):
        def one(p, carry):
            out[p, :, 0] = field[:, 2 * p]
            out[p, :, 1] = field[:, 2 * p + 1]
            right = field[:, lax.rem(2 * p + 2, NB)]
            left = field[:, lax.rem(2 * p + NB - 1, NB)]
            out[p, :, 2] = jnp.where(iota(right.shape, right.ndim - 1) < 64, right, left)
            return carry

        lax.fori_loop(0, NPX, one, 0)

    def block(ext, k):
        return ext.at[:, :, :, pl.ds(pl.multiple_of(k * 16, 16), 16), :]

    def turn(send, ext, k, ssem, rsem):
        return pltpu.make_async_remote_copy(
            src_ref=send.at[ypeer(k)], dst_ref=block(ext, px),
            send_sem=ssem.at[k], recv_sem=rsem.at[k],
            device_id={"px": ypeer(k)}, device_id_type=MESH,
        )

    def turned(send, ext, k, ssem, rsem):
        source = lax.rem(px + NPX - k, NPX)
        return pltpu.make_async_remote_copy(
            src_ref=send.at[source], dst_ref=block(ext, source),
            send_sem=ssem.at[k], recv_sem=rsem.at[k],
            device_id={"px": ypeer(k)}, device_id_type=MESH,
        )

    def start_turn(send, ext, ssem, rsem):
        def one(k, carry):
            turn(send, ext, k, ssem, rsem).start()
            return carry

        lax.fori_loop(1, NPX, one, 0)
        ext[:, :, :, pl.ds(pl.multiple_of(px * 16, 16), 16), :] = send[px]

    def end_turn(send, ext, ssem, rsem):
        def one(k, carry):
            turned(send, ext, k, ssem, rsem).wait_recv()
            return carry

        lax.fori_loop(1, NPX, one, 0)

    pl.semaphore_wait(barrier, NPX - 1 + NPY - 1)

    def edge(side):
        peer = ypeer(1 if side == 1 else NPX - 1)
        return pltpu.make_async_remote_copy(
            src_ref=cc.at[side], dst_ref=halo.at[side],
            send_sem=s_h.at[side], recv_sem=r_h.at[side],
            device_id={"px": peer}, device_id_type=MESH,
        )

    def route(buf, land, k, ssem, rsem):
        return pltpu.make_async_remote_copy(
            src_ref=buf.at[k], dst_ref=land.at[k],
            send_sem=ssem.at[k], recv_sem=rsem.at[k],
            device_id={"py": opeer(k)}, device_id_type=MESH,
        )

    slot = iota((CAP, L), 0).astype(f32)

    def gather(k):
        base = pl.multiple_of(opeer(k) * 8, 8)
        mine = keys[pl.ds(base, 8), :]
        for bl in range(8):
            pbuf[:, bl * L:(bl + 1) * L] = (slot == mine[bl:bl + 1, :]).astype(f32).astype(bf16)
        m = lax.dot_general(metaq[...], pbuf[...], NT, preferred_element_type=f32)
        meta = jnp.concatenate([m[0:1] + m[1:2] + m[2:3], m[4:5] * 32.0 + m[3:4]], axis=0)
        out = dot(pbuf[...], vals[...])
        return meta, out[:, 0:L] + out[:, L:2 * L], out[:, 2 * L:3 * L] + out[:, 3 * L:4 * L]

    def send_rows(k, carry):
        meta, w, wd = gather(k)
        sm[k] = meta
        sw[k] = w
        sd[k] = wd
        route(sm, rm, k, s_m, r_m).start()
        route(sw, rw, k, s_w, r_w).start()
        return carry

    lax.fori_loop(1, NPY, send_rows, 0)

    def send_data(k, carry):
        route(sd, rd, k, s_d, r_d).start()
        return carry

    lax.fori_loop(1, NPY, send_data, 0)

    meta, w, wd = gather(0)
    rm[0] = meta
    rw[0] = w
    rd[0] = wd

    for load in loads[6:]:
        load.wait()
    for j in range(2):
        tail = cc[j, 2, L - 8:L, :]
        cc[j, 2, L - 8:L, :] = jnp.where(iota((8, L), 0) < 7, tail, 0.0)
    lanes16 = iota((16, L), 1)
    for b in range(NB):
        tile = cyin[:, b * L:(b + 1) * L]
        if b == NB - 1:
            tile = jnp.where(lanes16 < L - 1, tile, 0.0)
        cyfield[0, b, 0] = tile

    def free_turn(send, ext, ssem, rsem):
        def one(k, carry):
            turn(send, ext, k, ssem, rsem).wait_send()
            return carry

        lax.fori_loop(1, NPX, one, 0)

    pack(cyfield, cysend)

    edge(0).start()
    edge(1).start()
    start_turn(cysend, cyx, s_c, r_c)

    for side in range(2):
        edge(side).wait_recv()
    lanes = iota((L, L), 1)
    for f in range(3):
        cc[2, f] = jnp.where(lanes < 64, halo[0, f], halo[1, f])
    end_turn(cysend, cyx, s_c, r_c)

    CH = 128

    def tiles(count, body, fields=(0, 1)):
        def one(j, carry):
            for f in fields:
                body(j, f)
            return carry

        for j in range(count):
            one(j, 0)

    def chunks(body, fields=(0, 1)):
        def one(i, carry):
            rows = pl.ds(pl.multiple_of(i * CH, CH), CH)
            for f in fields:
                body(f, rows)
            return carry

        lax.fori_loop(0, L // CH, one, 0)

    def bands_x(j, carry):
        for m, w in enumerate(band([cc[j, 2]], xshift)):
            wx[m, j] = w[0]
        return carry

    def bands_y(i, carry):
        rows = pl.ds(pl.multiple_of(i * 16, 16), 16)
        for m, w in enumerate(band([cyx[0, j, 0, rows, :] for j in range(3)], yshift)):
            for j in range(3):
                wy[m, j, rows, :] = w[j]
        return carry

    lax.fori_loop(0, 3, bands_x, 0)
    lax.fori_loop(0, 8, bands_y, 0)

    def sweep_x(v, j):
        return sweep(lambda m, _: wx[m, j], [v], xshift)[0]

    def sweep_y(v, rows, keep=3):
        return sweep(lambda m, j: wy[m, j, rows, :], v, yshift, keep)

    def first_x(j, f):
        ubuf[j, f] = sweep_x(cc[j, f], j)

    def first_y(f, rows):
        v = sweep_y([ubuf[j, f, rows, :] for j in range(3)], rows)
        for j in range(3):
            ubuf[j, f, rows, :] = v[j]

    tiles(3, first_x)
    chunks(first_y)

    pick = jnp.where(iota((8, L), 0) < 3, 1.0, 0.0).astype(bf16)
    target = iota((T, 4 * CAP), 0).astype(f32)

    def group(g, land, buf, ssem, rsem, with_meta, parts):
        for i in range(4):
            k = 4 * g + i

            @pl.when(k > 0)
            def _():
                if with_meta:
                    route(sm, rm, k, s_m, r_m).wait_recv()
                route(buf, land, k, ssem, rsem).wait_recv()

            rows = slice(i * CAP, (i + 1) * CAP)
            if with_meta:
                meta = rm[k]
                s = meta[0:1, :]
                hi = s.astype(bf16).astype(f32)
                mid = (s - hi).astype(bf16).astype(f32)
                three = jnp.concatenate([hi, mid, s - hi - mid, jnp.zeros((5, CAP), f32)], axis=0)
                s = lax.dot_general(three.astype(bf16), pick, TN, preferred_element_type=f32)
                shares_of[k] = s
                tid[0:1, rows] = meta[1:2, :]
            else:
                s = shares_of[k]
            v = land[k]
            va = v * (1.0 - s)
            vs = v * s
            terms = (va * (1.0 - s), vs * s, vs * (1.0 - s)) if parts == 3 else (va, vs)
            for n, term in enumerate(terms):
                hi, lo = split(term)
                rhs[rows, 2 * n * L:(2 * n + 1) * L] = hi
                rhs[rows, (2 * n + 1) * L:(2 * n + 2) * L] = lo
        if with_meta:
            onehot[g] = (target == tid[0:1, :]).astype(f32).astype(bf16)
        width = 2 * parts * L
        part = dot(onehot[g], rhs[:, 0:width])

        @pl.when(g == 0)
        def _():
            acc[:, 0:width] = part

        @pl.when(g > 0)
        def _():
            acc[:, 0:width] += part

    def w_group(g, carry):
        group(g, rw, sw, s_w, r_w, True, 3)
        return carry

    lax.fori_loop(0, 4, w_group, 0)

    def column(n):
        return acc[:, 2 * n * L:(2 * n + 1) * L] + acc[:, (2 * n + 1) * L:(2 * n + 2) * L]

    tfield[0] = (column(0) + pltpu.roll(column(1), 1, 0)).reshape(NB, 2, 16, L)
    tfield[1] = column(2).reshape(NB, 2, 16, L)
    pack(tfield, tsend)
    start_turn(tsend, text, s_t, r_t)

    def d_group(g, carry):
        group(g, rd, sd, s_d, r_d, False, 2)
        return carry

    lax.fori_loop(0, 4, d_group, 0)
    bfield[0] = (column(0) + pltpu.roll(column(1), 1, 0)).reshape(NB, 2, 16, L)

    def b_pack(f, p):
        right = bfield[0, lax.rem(2 * p + 2, NB), f]
        left = bfield[0, lax.rem(2 * p + NB - 1, NB), f]
        return [bfield[0, 2 * p, f], bfield[0, 2 * p + 1, f], jnp.where(lanes16 < 64, right, left)]

    def b_copy(f, k, source):
        return pltpu.make_async_remote_copy(
            src_ref=bsend.at[f, ypeer(k)],
            dst_ref=bext.at[f, :, pl.ds(pl.multiple_of(source * 16, 16), 16), :],
            send_sem=s_b.at[f, k], recv_sem=r_b.at[f, k],
            device_id={"px": ypeer(k)}, device_id_type=MESH,
        )

    for f in range(2):
        def b_send(k, carry, f=f):
            for j, tile in enumerate(b_pack(f, ypeer(k))):
                bsend[f, ypeer(k), j] = tile
            b_copy(f, k, px).start()
            return carry

        lax.fori_loop(1, NPX, b_send, 0)
    for f in range(2):
        for j, tile in enumerate(b_pack(f, px)):
            bext[f, j, pl.ds(pl.multiple_of(px * 16, 16), 16), :] = tile

    def drain_py(k, carry):
        route(sm, rm, k, s_m, r_m).wait_send()
        route(sw, rw, k, s_w, r_w).wait_send()
        route(sd, rd, k, s_d, r_d).wait_send()
        return carry

    for side in range(2):
        edge(side).wait_send()
    free_turn(cysend, cyx, s_c, r_c)
    end_turn(tsend, text, s_t, r_t)

    def spread(f, rows, keep=3):
        u = [ubuf[j, f, rows, :] for j in range(3)]
        return u, [tri(u[j], text[0, j, f, rows, :], text[1, j, f, rows, :]) for j in range(3)]

    def mid_chunk(f, rows):
        v = sweep_y(spread(f, rows)[1], rows)
        for j in range(3):
            gbuf[j, f, rows, :] = v[j]

    chunks(mid_chunk)

    def image_start(j, f):
        abuf[j, f] = cc[j, f] + sweep_x(gbuf[j, f], j)

    tiles(3, image_start)
    lax.fori_loop(1, NPY, drain_py, 0)
    free_turn(tsend, text, s_t, r_t)

    dots[...] = jnp.zeros_like(dots)

    def add_dot(n, a, b):
        dots[n] += jnp.sum((a * b).reshape(-1, 8, L), axis=0)

    def b_chunk(f, rows):
        v = sweep_y([bext[f, j, rows, :] for j in range(3)], rows)
        for j in range(3):
            gbuf[j, f, rows, :] = v[j]


    def residual_tile(j, f):
        r = sweep_x(gbuf[j, f], j) - abuf[j, f]
        rbuf[j, f] = r

        if j < 2:
            add_dot(0, r, r)

        ubuf[j, f] = sweep_x(r, j)


    def q_chunk(f, rows):
        u = sweep_y([ubuf[j, f, rows, :] for j in range(3)], rows)
        v = [tri(u[j], text[0, j, f, rows, :], text[1, j, f, rows, :]) for j in range(3)]
        for j in range(2):
            add_dot(1, u[j], v[j])
        v = sweep_y(v, rows)
        for j in range(3):
            gbuf[j, f, rows, :] = v[j]


    def q_tile(j, f):
        q = rbuf[j, f] + sweep_x(gbuf[j, f], j)
        qbuf[j, f] = q

        if j < 2:
            add_dot(2, q, q)

        ubuf[j, f] = sweep_x(q, j)


    def p_up(f, rows):
        u = sweep_y([ubuf[j, f, rows, :] for j in range(3)], rows)
        v = [tri(u[j], text[0, j, f, rows, :], text[1, j, f, rows, :]) for j in range(3)]
        for j in range(2):
            add_dot(3, u[j], v[j])
        for j in range(3):
            ubuf[j, f, rows, :] = v[j]

    for f in range(2):
        def b_wait(k, carry, f=f):
            b_copy(f, k, lax.rem(px + NPX - k, NPX)).wait_recv()
            return carry

        lax.fori_loop(1, NPX, b_wait, 0)
        chunks(b_chunk, (f,))
        tiles(3, residual_tile, (f,))
        chunks(q_chunk, (f,))
        tiles(3, q_tile, (f,))
        chunks(p_up, (f,))

    def p_down(f, rows):
        v = sweep_y([ubuf[j, f, rows, :] for j in range(3)], rows, 2)
        for j in range(2):
            gbuf[j, f, rows, :] = v[j]

    def p_tile(j, f):
        abuf[j, f] = qbuf[j, f] + sweep_x(gbuf[j, f], j)

    lines = [jnp.sum(dots[n], axis=0, keepdims=True) for n in range(4)]
    red1[0] = jnp.concatenate(lines + [jnp.zeros((4, L), f32)], axis=0)

    def sum1(k):
        return pltpu.make_async_remote_copy(
            src_ref=red1.at[0], dst_ref=red1.at[k], send_sem=s_1.at[k], recv_sem=r_1.at[k],
            device_id={"px": ypeer(k)}, device_id_type=MESH,
        )

    def sum2(k):
        return pltpu.make_async_remote_copy(
            src_ref=red2.at[0], dst_ref=red2.at[k], send_sem=s_2.at[k], recv_sem=r_2.at[k],
            device_id={"py": opeer(k)}, device_id_type=MESH,
        )

    def put(n, buf, out):
        return [
            pltpu.make_async_copy(buf.at[j], out.at[:, :, j * L:(j + 1) * L], s_o.at[2 * n + j])
            for j in range(2)
        ]

    def merge(count, send, buf):
        for k in range(1, count):
            send(k).wait_recv()
        total = buf[0]
        for k in range(1, count):
            total = total + buf[k]
        return total

    for k in range(1, NPX):
        sum1(k).start()
    outs = put(0, rbuf, o_r) + put(1, qbuf, o_q)
    for copy in outs:
        copy.start()
    chunks(p_down)
    for f in range(2):
        def b_free(k, carry, f=f):
            b_copy(f, k, px).wait_send()
            return carry

        lax.fori_loop(1, NPX, b_free, 0)
    red2[0] = merge(NPX, sum1, red1)
    for k in range(1, NPY):
        sum2(k).start()
    for k in range(1, NPX):
        sum1(k).wait_send()
    tiles(2, p_tile)
    last = put(2, abuf, o_p)
    for copy in last:
        copy.start()
    total = merge(NPY, sum2, red2)
    sums = jnp.sum(total, axis=1, keepdims=True)
    rr, gain, qq, gain2 = [sums[n:n + 1, :] for n in range(4)]
    rq = rr + gain
    qp = qq + gain2
    alpha = rr / rq
    new = alpha * (alpha * qq) - rr
    beta = new / rr
    grow = 1.0 + beta
    alpha2 = new / (grow * grow * rq - 2.0 * alpha * grow * qq + alpha * alpha * qp)
    kr = alpha + alpha2 * grow
    kq = -alpha2 * alpha

    o_k[0:1, :] = jnp.broadcast_to(kr, (1, L))
    o_k[1:2, :] = jnp.broadcast_to(kq, (1, L))
    for copy in outs + last:
        copy.wait()
    for k in range(1, NPY):
        sum2(k).wait_send()


def finish(c, r, q, p, k, control, residual):
    kr = k[0:1, 0:1]
    kq = k[1:2, 0:1]
    for f in range(2):
        control[f] = c[f] + kr * r[f] + kq * q[f]
        residual[f] = r[f] - kr * q[f] - kq * p[f]


def shards(control_start, coef_x, coef_y, innovation, obs_weight, interp, obs_owner, cell_key, stencil):
    dma = pltpu.SemaphoreType.DMA
    vm = pltpu.VMEM
    field = vm((3, 2, L, L), f32)
    scratch = [
        vm((8, L), jnp.int32), vm((8, L), jnp.int32), vm((8, L), jnp.int32), vm((8, L), f32),
        vm((ROWS, L), f32), vm((ROWS, L), f32), vm((16, NB * L), f32), dma((11,)),
        vm((2 * M + 1, 3, L, L), f32), vm((2 * M + 1, 3, L, L), f32),
        vm((L, L), f32), vm((ROWS, 4 * L), bf16), vm((8, ROWS), bf16), vm((CAP, ROWS), bf16),
        vm((NPY, CAP, L), f32), vm((NPY, CAP, L), f32), vm((NPY, 2, CAP), f32),
        vm((NPY, CAP, L), f32), vm((NPY, CAP, L), f32), vm((NPY, 2, CAP), f32),
        vm((4 * CAP, 6 * L), bf16), vm((8, 4 * CAP), f32), vm((T, 6 * L), f32),
        vm((2, NB, 2, 16, L), f32), vm((NPX, 2, 3, 2, 16, L), f32),
        vm((1, NB, 2, 16, L), f32), vm((2, NPX, 3, 16, L), f32),
        vm((1, NB, 1, 16, L), f32), vm((NPX, 1, 3, 1, 16, L), f32),
        vm((3, 3, L, L), f32), vm((2, 3, L, L), f32),
        vm((2, 3, 2, L, L), f32), vm((2, 3, L, L), f32), vm((1, 3, 1, L, L), f32),
        field, field, field, field, field,
        vm((4, 8, L), f32), vm((NPX, 8, L), f32), vm((NPY, 8, L), f32),
        vm((4, T, 4 * CAP), bf16), vm((NPY, CAP, L), f32),
        dma((NPY,)), dma((NPY,)), dma((NPY,)), dma((NPY,)), dma((NPY,)), dma((NPY,)),
        dma((NPX,)), dma((NPX,)), dma((2, NPX)), dma((2, NPX)), dma((NPX,)), dma((NPX,)),
        dma((2,)), dma((2,)), dma((NPX,)), dma((NPX,)), dma((NPY,)), dma((NPY,)), dma((6,)),
    ]
    out = jax.ShapeDtypeStruct((2, L, 2 * L), f32)
    r, q, p, k = pl.pallas_call(
        kernel,
        out_shape=(out, out, out, jax.ShapeDtypeStruct((2, L), f32)),
        in_specs=[pl.BlockSpec(memory_space=pltpu.HBM)] * 9,
        out_specs=(pl.BlockSpec(memory_space=pltpu.HBM),) * 3 + (pl.BlockSpec(memory_space=pltpu.VMEM),),
        scratch_shapes=scratch,
        compiler_params=pltpu.CompilerParams(
            collective_id=0, has_side_effects=True, vmem_limit_bytes=60 * 1024 * 1024
        ),
        name="assimilate",
    )(
        obs_owner.reshape(8, L), cell_key.reshape(8, L), stencil.reshape(8, L), interp.reshape(8, L),
        innovation, obs_weight, control_start.reshape(2, L, 2 * L), coef_x.reshape(L, 2 * L),
        coef_y.reshape(16, NB * L),
    )
    shape = control_start.shape
    control, residual = pl.pallas_call(
        finish, out_shape=(out, out), name="finish",
        in_specs=[pl.BlockSpec(memory_space=pltpu.VMEM)] * 5,
        compiler_params=pltpu.CompilerParams(vmem_limit_bytes=60 * 1024 * 1024),
    )(control_start.reshape(2, L, 2 * L), r, q, p, k)
    return control.reshape(shape), residual.reshape(shape)


def solution(mesh):
    return jax.shard_map(
        shards,
        mesh=mesh,
        in_specs=(
            P(None, "py", None, "px"),
            P("py", None, "px"),
            P("py", "px", None),
            P(("px", "py"), None),
            P(("px", "py"), None),
            P(("px", "py")),
            P(("px", "py"), None),
            P(("px", "py")),
            P(("px", "py")),
        ),
        out_specs=(P(None, "py", None, "px"), P(None, "py", None, "px")),
        check_vma=False,
    )
```

```python
import jax
import jax.numpy as jnp
from jax import lax
from jax.experimental import pallas as pl
from jax.experimental.pallas import tpu as pltpu
from jax.sharding import PartitionSpec as P

NPX = 8
NPY = 16
CAP = 192
ROWS = 1024
L = 128
M = 4
NB = 16
T = 512
f32 = jnp.float32
bf16 = jnp.bfloat16
MESH = pl.DeviceIdType.MESH
NT = (((1,), (1,)), ((), ()))
TN = (((0,), (0,)), ((), ()))


def dot(a, b):
    return jnp.dot(a, b, preferred_element_type=f32)


def iota(shape, axis):
    return lax.broadcasted_iota(jnp.int32, shape, axis)


def split(v):
    hi = v.astype(bf16)
    return hi, (v - hi.astype(f32)).astype(bf16)


def xshift(v, k):
    return [pltpu.roll(t, (-k) % L, 0) for t in v] if k else v


def yshift(v, k):
    if k == 0:
        return v
    lane = iota(v[0].shape, 1)
    r = [pltpu.roll(t, (-k) % L, 1) for t in v]
    n = len(v)
    if k > 0:
        return [jnp.where(lane < L - k, r[j], r[(j + 1) % n]) for j in range(n)]
    return [jnp.where(lane >= -k, r[j], r[(j + n - 1) % n]) for j in range(n)]


def mul(a, b):
    return [x * y for x, y in zip(a, b)]


def add(*terms):
    total = terms[0]
    for t in terms[1:]:
        total = [x + y for x, y in zip(total, t)]
    return total


def band(c, shift):
    a = shift(c, -1)
    d = [1.0 - x - y for x, y in zip(c, a)]
    p0 = add(mul(d, d), mul(c, c), mul(a, a))
    p1 = mul(c, add(d, shift(d, 1)))
    p2 = mul(c, shift(c, 1))
    n1, n2 = shift(p1, -1), shift(p2, -2)
    up1 = shift(p1, 1)
    b0 = add(mul(p0, p0), mul(p1, p1), mul(p2, p2), mul(n1, n1), mul(n2, n2))
    b1 = add(mul(p1, add(p0, shift(p0, 1))), mul(p2, up1), mul(n1, shift(p2, -1)))
    b2 = add(mul(p0, p2), mul(p1, up1), mul(p2, shift(p0, 2)))
    b3 = add(mul(p1, shift(p2, 1)), mul(p2, shift(p1, 2)))
    b4 = mul(p2, shift(p2, 2))
    return [shift(b4, -4), shift(b3, -3), shift(b2, -2), shift(b1, -1), b0, b1, b2, b3, b4]


def sweep(w, v, shift, keep=3):
    total = None
    for m in range(2 * M + 1):
        moved = shift(v, m - M)[:keep]
        term = [w(m, j) * t for j, t in enumerate(moved)]
        total = term if total is None else add(total, term)
    return total


def tri(u, d, e):
    eu = e * u
    return d * u + e * pltpu.roll(u, u.shape[0] - 1, 0) + pltpu.roll(eu, 1, 0)


def kernel(
    h_own, h_key, h_sten, h_itp, h_inn, h_wgt, h_c, h_cx, h_cy, o_r, o_q, o_p, o_k,
    own, key, sten, itp, inn, wgt, cyin, s_in, wx, wy,
    keys, vals, metaq, pbuf, sw, sd, sm, rw, rd, rm, rhs, tid, acc,
    tfield, tsend, bfield, bsend, cyfield, cysend, cc, halo, text, bext, cyx,
    ubuf, gbuf, abuf, rbuf, qbuf, dots, red1, red2, onehot, shares_of,
    s_m, s_w, s_d, r_m, r_w, r_d, s_t, r_t, s_b, r_b, s_c, r_c, s_h, r_h, s_1, r_1, s_2, r_2, s_o,
):
    px = lax.axis_index("px")
    py = lax.axis_index("py")

    def ypeer(k):
        return lax.rem(px + k, NPX)

    def opeer(k):
        k = lax.rem(k + lax.rem(px, 2) * (2 * NPY - 2 * k), NPY)
        x = lax.rem(py // 4 + lax.rem(k, 4), 4)
        z = lax.rem(lax.rem(py, 4) + k // 4 + 4 - lax.rem(k, 4), 4)
        return x * 4 + z

    loads = [(h_own, own), (h_key, key), (h_sten, sten), (h_itp, itp), (h_wgt, wgt), (h_inn, inn), (h_cy, cyin)]
    for j in range(2):
        lanes = slice(j * L, (j + 1) * L)
        loads.append((h_c.at[:, :, lanes], cc.at[j, 0:2]))
        loads.append((h_cx.at[:, lanes], cc.at[j, 2]))
    loads = [pltpu.make_async_copy(a, b, s_in.at[n]) for n, (a, b) in enumerate(loads)]
    for load in loads:
        load.start()

    barrier = pltpu.get_barrier_semaphore()

    def greet_px(k, carry):
        pl.semaphore_signal(barrier, inc=1, device_id={"px": ypeer(k)}, device_id_type=MESH)
        return carry

    def greet_py(k, carry):
        pl.semaphore_signal(barrier, inc=1, device_id={"py": opeer(k)}, device_id_type=MESH)
        return carry

    for k in range(1, NPX):
        greet_px(k, 0)
    for k in range(1, NPY):
        greet_py(k, 0)

    for n in range(4):
        loads[n].wait()
    row = iota((L, L), 0)
    col = iota((L, L), 1)
    owner = own[...]
    hit = jnp.concatenate([(owner == d).astype(f32) for d in range(NPY)], axis=0)
    hit16 = hit.astype(bf16)
    upper = (row < col).astype(f32).astype(bf16)
    before = ((row // 8 == col // 8) & (col < row)).astype(f32).astype(bf16)
    inside = dot(hit16, upper)
    count = dot(hit16, jnp.ones((L, L), bf16))
    keys[...] = jnp.where(hit > 0.5, inside + dot(before, count.astype(bf16)), -1.0)

    share = itp[...]
    s_hi, rest = split(share)
    s_hi = s_hi.astype(f32)
    rest = share - s_hi
    s_mid = rest.astype(bf16).astype(f32)
    s_lo = rest - s_mid
    cell = key[...]
    fx = ((cell // NB) * 16 + sten[...]).astype(f32)
    seg = lax.rem(cell, NB).astype(f32)
    zero = jnp.zeros((3, L), f32)
    for bl in range(8):
        pick = [t[bl:bl + 1, :] for t in (s_hi, s_mid, s_lo, fx, seg)] + [zero]
        metaq[:, bl * L:(bl + 1) * L] = jnp.concatenate(pick, axis=0).astype(bf16)

    loads[4].wait()
    loads[5].wait()

    def cut(i, carry):
        rows = pl.ds(pl.multiple_of(i * L, L), L)
        w = wgt[rows, :]
        hi, lo = split(w)
        vals[rows, 0:L] = hi
        vals[rows, L:2 * L] = lo
        hi, lo = split(w * inn[rows, :])
        vals[rows, 2 * L:3 * L] = hi
        vals[rows, 3 * L:4 * L] = lo
        return carry

    lax.fori_loop(0, 8, cut, 0)

    def pack(field, out):
        def one(p, carry):
            out[p, :, 0] = field[:, 2 * p]
            out[p, :, 1] = field[:, 2 * p + 1]
            right = field[:, lax.rem(2 * p + 2, NB)]
            left = field[:, lax.rem(2 * p + NB - 1, NB)]
            out[p, :, 2] = jnp.where(iota(right.shape, right.ndim - 1) < 64, right, left)
            return carry

        lax.fori_loop(0, NPX, one, 0)

    def block(ext, k):
        return ext.at[:, :, :, pl.ds(pl.multiple_of(k * 16, 16), 16), :]

    def turn(send, ext, k, ssem, rsem):
        return pltpu.make_async_remote_copy(
            src_ref=send.at[ypeer(k)], dst_ref=block(ext, px),
            send_sem=ssem.at[k], recv_sem=rsem.at[k],
            device_id={"px": ypeer(k)}, device_id_type=MESH,
        )

    def turned(send, ext, k, ssem, rsem):
        source = lax.rem(px + NPX - k, NPX)
        return pltpu.make_async_remote_copy(
            src_ref=send.at[source], dst_ref=block(ext, source),
            send_sem=ssem.at[k], recv_sem=rsem.at[k],
            device_id={"px": ypeer(k)}, device_id_type=MESH,
        )

    def start_turn(send, ext, ssem, rsem):
        def one(k, carry):
            turn(send, ext, k, ssem, rsem).start()
            return carry

        lax.fori_loop(1, NPX, one, 0)
        ext[:, :, :, pl.ds(pl.multiple_of(px * 16, 16), 16), :] = send[px]

    def end_turn(send, ext, ssem, rsem):
        def one(k, carry):
            turned(send, ext, k, ssem, rsem).wait_recv()
            return carry

        lax.fori_loop(1, NPX, one, 0)


    def edge(side):
        peer = ypeer(1 if side == 1 else NPX - 1)
        return pltpu.make_async_remote_copy(
            src_ref=cc.at[side], dst_ref=halo.at[side],
            send_sem=s_h.at[side], recv_sem=r_h.at[side],
            device_id={"px": peer}, device_id_type=MESH,
        )

    def route(buf, land, k, ssem, rsem):
        return pltpu.make_async_remote_copy(
            src_ref=buf.at[k], dst_ref=land.at[k],
            send_sem=ssem.at[k], recv_sem=rsem.at[k],
            device_id={"py": opeer(k)}, device_id_type=MESH,
        )

    slot = iota((CAP, L), 0).astype(f32)

    def gather(k):
        base = pl.multiple_of(opeer(k) * 8, 8)
        mine = keys[pl.ds(base, 8), :]
        for bl in range(8):
            pbuf[:, bl * L:(bl + 1) * L] = (slot == mine[bl:bl + 1, :]).astype(f32).astype(bf16)
        m = lax.dot_general(metaq[...], pbuf[...], NT, preferred_element_type=f32)
        meta = jnp.concatenate([m[0:1] + m[1:2] + m[2:3], m[4:5] * 32.0 + m[3:4]], axis=0)
        out = dot(pbuf[...], vals[...])
        return meta, out[:, 0:L] + out[:, L:2 * L], out[:, 2 * L:3 * L] + out[:, 3 * L:4 * L]

    def fill_rows(k, carry):
        meta, w, wd = gather(k)
        sm[k] = meta
        sw[k] = w
        sd[k] = wd
        return carry

    lax.fori_loop(1, 6, fill_rows, 0)
    pl.semaphore_wait(barrier, NPX - 1 + NPY - 1)

    def start_rows(k, carry):
        route(sm, rm, k, s_m, r_m).start()
        route(sw, rw, k, s_w, r_w).start()
        return carry

    lax.fori_loop(1, 6, start_rows, 0)

    def send_rows(k, carry):
        meta, w, wd = gather(k)
        sm[k] = meta
        sw[k] = w
        sd[k] = wd
        route(sm, rm, k, s_m, r_m).start()
        route(sw, rw, k, s_w, r_w).start()
        return carry

    lax.fori_loop(6, NPY, send_rows, 0)

    def send_data(k, carry):
        route(sd, rd, k, s_d, r_d).start()
        return carry

    lax.fori_loop(1, NPY, send_data, 0)

    meta, w, wd = gather(0)
    rm[0] = meta
    rw[0] = w
    rd[0] = wd

    for load in loads[6:]:
        load.wait()
    for j in range(2):
        tail = cc[j, 2, L - 8:L, :]
        cc[j, 2, L - 8:L, :] = jnp.where(iota((8, L), 0) < 7, tail, 0.0)
    lanes16 = iota((16, L), 1)
    for b in range(NB):
        tile = cyin[:, b * L:(b + 1) * L]
        if b == NB - 1:
            tile = jnp.where(lanes16 < L - 1, tile, 0.0)
        cyfield[0, b, 0] = tile

    def free_turn(send, ext, ssem, rsem):
        def one(k, carry):
            turn(send, ext, k, ssem, rsem).wait_send()
            return carry

        lax.fori_loop(1, NPX, one, 0)

    pack(cyfield, cysend)

    edge(0).start()
    edge(1).start()
    start_turn(cysend, cyx, s_c, r_c)

    for side in range(2):
        edge(side).wait_recv()
    lanes = iota((L, L), 1)
    for f in range(3):
        cc[2, f] = jnp.where(lanes < 64, halo[0, f], halo[1, f])
    end_turn(cysend, cyx, s_c, r_c)

    CH = 128

    def tiles(count, body, fields=(0, 1)):
        def one(j, carry):
            for f in fields:
                body(j, f)
            return carry

        for j in range(count):
            one(j, 0)

    def chunks(body, fields=(0, 1)):
        def one(i, carry):
            rows = pl.ds(pl.multiple_of(i * CH, CH), CH)
            for f in fields:
                body(f, rows)
            return carry

        lax.fori_loop(0, L // CH, one, 0)

    def bands_x(j, carry):
        for m, w in enumerate(band([cc[j, 2]], xshift)):
            wx[m, j] = w[0]
        return carry

    def bands_y(i, carry):
        rows = pl.ds(pl.multiple_of(i * 16, 16), 16)
        for m, w in enumerate(band([cyx[0, j, 0, rows, :] for j in range(3)], yshift)):
            for j in range(3):
                wy[m, j, rows, :] = w[j]
        return carry

    lax.fori_loop(0, 3, bands_x, 0)
    lax.fori_loop(0, 8, bands_y, 0)

    def sweep_x(v, j):
        return sweep(lambda m, _: wx[m, j], [v], xshift)[0]

    def sweep_y(v, rows, keep=3):
        return sweep(lambda m, j: wy[m, j, rows, :], v, yshift, keep)

    def first_x(j, f):
        ubuf[j, f] = sweep_x(cc[j, f], j)

    def first_y(f, rows):
        v = sweep_y([ubuf[j, f, rows, :] for j in range(3)], rows)
        for j in range(3):
            ubuf[j, f, rows, :] = v[j]

    tiles(3, first_x)
    chunks(first_y)

    pick = jnp.where(iota((8, L), 0) < 3, 1.0, 0.0).astype(bf16)
    target = iota((T, 4 * CAP), 0).astype(f32)

    def group(g, land, buf, ssem, rsem, with_meta, parts):
        for i in range(4):
            k = 4 * g + i

            @pl.when(k > 0)
            def _():
                if with_meta:
                    route(sm, rm, k, s_m, r_m).wait_recv()
                route(buf, land, k, ssem, rsem).wait_recv()

            rows = slice(i * CAP, (i + 1) * CAP)
            if with_meta:
                meta = rm[k]
                s = meta[0:1, :]
                hi = s.astype(bf16).astype(f32)
                mid = (s - hi).astype(bf16).astype(f32)
                three = jnp.concatenate([hi, mid, s - hi - mid, jnp.zeros((5, CAP), f32)], axis=0)
                s = lax.dot_general(three.astype(bf16), pick, TN, preferred_element_type=f32)
                shares_of[k] = s
                tid[0:1, rows] = meta[1:2, :]
            else:
                s = shares_of[k]
            v = land[k]
            va = v * (1.0 - s)
            vs = v * s
            terms = (va * (1.0 - s), vs * s, vs * (1.0 - s)) if parts == 3 else (va, vs)
            for n, term in enumerate(terms):
                hi, lo = split(term)
                rhs[rows, 2 * n * L:(2 * n + 1) * L] = hi
                rhs[rows, (2 * n + 1) * L:(2 * n + 2) * L] = lo
        if with_meta:
            onehot[g] = (target == tid[0:1, :]).astype(f32).astype(bf16)
        width = 2 * parts * L
        part = dot(onehot[g], rhs[:, 0:width])

        @pl.when(g == 0)
        def _():
            acc[:, 0:width] = part

        @pl.when(g > 0)
        def _():
            acc[:, 0:width] += part

    def w_group(g, carry):
        group(g, rw, sw, s_w, r_w, True, 3)
        return carry

    lax.fori_loop(0, 4, w_group, 0)

    def column(n):
        return acc[:, 2 * n * L:(2 * n + 1) * L] + acc[:, (2 * n + 1) * L:(2 * n + 2) * L]

    tfield[0] = (column(0) + pltpu.roll(column(1), 1, 0)).reshape(NB, 2, 16, L)
    tfield[1] = column(2).reshape(NB, 2, 16, L)
    pack(tfield, tsend)
    start_turn(tsend, text, s_t, r_t)

    def d_group(g, carry):
        group(g, rd, sd, s_d, r_d, False, 2)
        return carry

    lax.fori_loop(0, 4, d_group, 0)
    bfield[0] = (column(0) + pltpu.roll(column(1), 1, 0)).reshape(NB, 2, 16, L)

    def b_pack(f, p):
        right = bfield[0, lax.rem(2 * p + 2, NB), f]
        left = bfield[0, lax.rem(2 * p + NB - 1, NB), f]
        return [bfield[0, 2 * p, f], bfield[0, 2 * p + 1, f], jnp.where(lanes16 < 64, right, left)]

    def b_copy(f, k, source):
        return pltpu.make_async_remote_copy(
            src_ref=bsend.at[f, ypeer(k)],
            dst_ref=bext.at[f, :, pl.ds(pl.multiple_of(source * 16, 16), 16), :],
            send_sem=s_b.at[f, k], recv_sem=r_b.at[f, k],
            device_id={"px": ypeer(k)}, device_id_type=MESH,
        )

    for f in range(2):
        def b_send(k, carry, f=f):
            for j, tile in enumerate(b_pack(f, ypeer(k))):
                bsend[f, ypeer(k), j] = tile
            b_copy(f, k, px).start()
            return carry

        for k in (4, 3, 5, 2, 6, 1, 7):
            b_send(k, 0)
    for f in range(2):
        for j, tile in enumerate(b_pack(f, px)):
            bext[f, j, pl.ds(pl.multiple_of(px * 16, 16), 16), :] = tile

    def drain_py(k, carry):
        route(sm, rm, k, s_m, r_m).wait_send()
        route(sw, rw, k, s_w, r_w).wait_send()
        route(sd, rd, k, s_d, r_d).wait_send()
        return carry

    for side in range(2):
        edge(side).wait_send()
    free_turn(cysend, cyx, s_c, r_c)
    end_turn(tsend, text, s_t, r_t)

    def spread(f, rows, keep=3):
        u = [ubuf[j, f, rows, :] for j in range(3)]
        return u, [tri(u[j], text[0, j, f, rows, :], text[1, j, f, rows, :]) for j in range(3)]

    def mid_chunk(f, rows):
        v = sweep_y(spread(f, rows)[1], rows)
        for j in range(3):
            gbuf[j, f, rows, :] = v[j]

    chunks(mid_chunk)

    def image_start(j, f):
        abuf[j, f] = cc[j, f] + sweep_x(gbuf[j, f], j)

    tiles(3, image_start)
    lax.fori_loop(1, NPY, drain_py, 0)
    free_turn(tsend, text, s_t, r_t)

    dots[...] = jnp.zeros_like(dots)

    def add_dot(n, a, b):
        dots[n] += jnp.sum((a * b).reshape(-1, 8, L), axis=0)

    def b_chunk(f, rows):
        v = sweep_y([bext[f, j, rows, :] for j in range(3)], rows)
        for j in range(3):
            gbuf[j, f, rows, :] = v[j]


    def residual_tile(j, f):
        r = sweep_x(gbuf[j, f], j) - abuf[j, f]
        rbuf[j, f] = r

        if j < 2:
            add_dot(0, r, r)

        ubuf[j, f] = sweep_x(r, j)


    def q_chunk(f, rows):
        u = sweep_y([ubuf[j, f, rows, :] for j in range(3)], rows)
        v = [tri(u[j], text[0, j, f, rows, :], text[1, j, f, rows, :]) for j in range(3)]
        for j in range(2):
            add_dot(1, u[j], v[j])
        v = sweep_y(v, rows)
        for j in range(3):
            gbuf[j, f, rows, :] = v[j]


    def q_tile(j, f):
        q = rbuf[j, f] + sweep_x(gbuf[j, f], j)
        qbuf[j, f] = q

        if j < 2:
            add_dot(2, q, q)

        ubuf[j, f] = sweep_x(q, j)


    def p_up(f, rows):
        u = sweep_y([ubuf[j, f, rows, :] for j in range(3)], rows)
        v = [tri(u[j], text[0, j, f, rows, :], text[1, j, f, rows, :]) for j in range(3)]
        for j in range(2):
            add_dot(3, u[j], v[j])
        for j in range(3):
            ubuf[j, f, rows, :] = v[j]

    for f in range(2):
        def b_wait(k, carry, f=f):
            b_copy(f, k, lax.rem(px + NPX - k, NPX)).wait_recv()
            return carry

        lax.fori_loop(1, NPX, b_wait, 0)
        chunks(b_chunk, (f,))
        tiles(3, residual_tile, (f,))
        chunks(q_chunk, (f,))
        tiles(3, q_tile, (f,))
        chunks(p_up, (f,))

    def p_down(f, rows):
        v = sweep_y([ubuf[j, f, rows, :] for j in range(3)], rows, 2)
        for j in range(2):
            gbuf[j, f, rows, :] = v[j]

    def p_tile(j, f):
        abuf[j, f] = qbuf[j, f] + sweep_x(gbuf[j, f], j)

    lines = [jnp.sum(dots[n], axis=0, keepdims=True) for n in range(4)]
    red1[0] = jnp.concatenate(lines + [jnp.zeros((4, L), f32)], axis=0)

    def sum1(k):
        return pltpu.make_async_remote_copy(
            src_ref=red1.at[0], dst_ref=red1.at[k], send_sem=s_1.at[k], recv_sem=r_1.at[k],
            device_id={"px": ypeer(k)}, device_id_type=MESH,
        )

    def sum2(k):
        return pltpu.make_async_remote_copy(
            src_ref=red2.at[0], dst_ref=red2.at[k], send_sem=s_2.at[k], recv_sem=r_2.at[k],
            device_id={"py": opeer(k)}, device_id_type=MESH,
        )

    def put(n, buf, out):
        return [
            pltpu.make_async_copy(buf.at[j], out.at[:, :, j * L:(j + 1) * L], s_o.at[2 * n + j])
            for j in range(2)
        ]

    def merge(count, send, buf):
        for k in range(1, count):
            send(k).wait_recv()
        total = buf[0]
        for k in range(1, count):
            total = total + buf[k]
        return total

    for k in range(1, NPX):
        sum1(k).start()
    outs = put(0, rbuf, o_r) + put(1, qbuf, o_q)
    for copy in outs:
        copy.start()
    chunks(p_down)
    for f in range(2):
        def b_free(k, carry, f=f):
            b_copy(f, k, px).wait_send()
            return carry

        lax.fori_loop(1, NPX, b_free, 0)
    red2[0] = merge(NPX, sum1, red1)
    for k in range(1, NPY):
        sum2(k).start()
    for k in range(1, NPX):
        sum1(k).wait_send()
    tiles(2, p_tile)
    last = put(2, abuf, o_p)
    for copy in last:
        copy.start()
    total = merge(NPY, sum2, red2)
    sums = jnp.sum(total, axis=1, keepdims=True)
    rr, gain, qq, gain2 = [sums[n:n + 1, :] for n in range(4)]
    rq = rr + gain
    qp = qq + gain2
    alpha = rr / rq
    new = alpha * (alpha * qq) - rr
    beta = new / rr
    grow = 1.0 + beta
    alpha2 = new / (grow * grow * rq - 2.0 * alpha * grow * qq + alpha * alpha * qp)
    kr = alpha + alpha2 * grow
    kq = -alpha2 * alpha

    o_k[0:1, :] = jnp.broadcast_to(kr, (1, L))
    o_k[1:2, :] = jnp.broadcast_to(kq, (1, L))
    for copy in outs + last:
        copy.wait()
    for k in range(1, NPY):
        sum2(k).wait_send()


def finish(c, r, q, p, k, control, residual):
    kr = k[0:1, 0:1]
    kq = k[1:2, 0:1]
    for f in range(2):
        control[f] = c[f] + kr * r[f] + kq * q[f]
        residual[f] = r[f] - kr * q[f] - kq * p[f]


def shards(control_start, coef_x, coef_y, innovation, obs_weight, interp, obs_owner, cell_key, stencil):
    dma = pltpu.SemaphoreType.DMA
    vm = pltpu.VMEM
    field = vm((3, 2, L, L), f32)
    scratch = [
        vm((8, L), jnp.int32), vm((8, L), jnp.int32), vm((8, L), jnp.int32), vm((8, L), f32),
        vm((ROWS, L), f32), vm((ROWS, L), f32), vm((16, NB * L), f32), dma((11,)),
        vm((2 * M + 1, 3, L, L), f32), vm((2 * M + 1, 3, L, L), f32),
        vm((L, L), f32), vm((ROWS, 4 * L), bf16), vm((8, ROWS), bf16), vm((CAP, ROWS), bf16),
        vm((NPY, CAP, L), f32), vm((NPY, CAP, L), f32), vm((NPY, 2, CAP), f32),
        vm((NPY, CAP, L), f32), vm((NPY, CAP, L), f32), vm((NPY, 2, CAP), f32),
        vm((4 * CAP, 6 * L), bf16), vm((8, 4 * CAP), f32), vm((T, 6 * L), f32),
        vm((2, NB, 2, 16, L), f32), vm((NPX, 2, 3, 2, 16, L), f32),
        vm((1, NB, 2, 16, L), f32), vm((2, NPX, 3, 16, L), f32),
        vm((1, NB, 1, 16, L), f32), vm((NPX, 1, 3, 1, 16, L), f32),
        vm((3, 3, L, L), f32), vm((2, 3, L, L), f32),
        vm((2, 3, 2, L, L), f32), vm((2, 3, L, L), f32), vm((1, 3, 1, L, L), f32),
        field, field, field, field, field,
        vm((4, 8, L), f32), vm((NPX, 8, L), f32), vm((NPY, 8, L), f32),
        vm((4, T, 4 * CAP), bf16), vm((NPY, CAP, L), f32),
        dma((NPY,)), dma((NPY,)), dma((NPY,)), dma((NPY,)), dma((NPY,)), dma((NPY,)),
        dma((NPX,)), dma((NPX,)), dma((2, NPX)), dma((2, NPX)), dma((NPX,)), dma((NPX,)),
        dma((2,)), dma((2,)), dma((NPX,)), dma((NPX,)), dma((NPY,)), dma((NPY,)), dma((6,)),
    ]
    out = jax.ShapeDtypeStruct((2, L, 2 * L), f32)
    r, q, p, k = pl.pallas_call(
        kernel,
        out_shape=(out, out, out, jax.ShapeDtypeStruct((2, L), f32)),
        in_specs=[pl.BlockSpec(memory_space=pltpu.HBM)] * 9,
        out_specs=(pl.BlockSpec(memory_space=pltpu.HBM),) * 3 + (pl.BlockSpec(memory_space=pltpu.VMEM),),
        scratch_shapes=scratch,
        compiler_params=pltpu.CompilerParams(
            collective_id=0, has_side_effects=True, vmem_limit_bytes=60 * 1024 * 1024
        ),
        name="assimilate",
    )(
        obs_owner.reshape(8, L), cell_key.reshape(8, L), stencil.reshape(8, L), interp.reshape(8, L),
        innovation, obs_weight, control_start.reshape(2, L, 2 * L), coef_x.reshape(L, 2 * L),
        coef_y.reshape(16, NB * L),
    )
    shape = control_start.shape
    control, residual = pl.pallas_call(
        finish, out_shape=(out, out), name="finish",
        in_specs=[pl.BlockSpec(memory_space=pltpu.VMEM)] * 5,
        compiler_params=pltpu.CompilerParams(vmem_limit_bytes=60 * 1024 * 1024),
    )(control_start.reshape(2, L, 2 * L), r, q, p, k)
    return control.reshape(shape), residual.reshape(shape)


def solution(mesh):
    return jax.shard_map(
        shards,
        mesh=mesh,
        in_specs=(
            P(None, "py", None, "px"),
            P("py", None, "px"),
            P("py", "px", None),
            P(("px", "py"), None),
            P(("px", "py"), None),
            P(("px", "py")),
            P(("px", "py"), None),
            P(("px", "py")),
            P(("px", "py")),
        ),
        out_specs=(P(None, "py", None, "px"), P(None, "py", None, "px")),
        check_vma=False,
    )
```

```python
import jax
import jax.numpy as jnp
from jax import lax
from jax.experimental import pallas as pl
from jax.experimental.pallas import tpu as pltpu
from jax.sharding import PartitionSpec as P

NPX = 8
NPY = 16
CAP = 192
ROWS = 1024
L = 128
M = 4
NB = 16
T = 512
f32 = jnp.float32
bf16 = jnp.bfloat16
MESH = pl.DeviceIdType.MESH
NT = (((1,), (1,)), ((), ()))
TN = (((0,), (0,)), ((), ()))


def dot(a, b):
    return jnp.dot(a, b, preferred_element_type=f32)


def iota(shape, axis):
    return lax.broadcasted_iota(jnp.int32, shape, axis)


def split(v):
    hi = v.astype(bf16)
    return hi, (v - hi.astype(f32)).astype(bf16)


def xshift(v, k):
    return [pltpu.roll(t, (-k) % L, 0) for t in v] if k else v


def yshift(v, k):
    if k == 0:
        return v
    lane = iota(v[0].shape, 1)
    r = [pltpu.roll(t, (-k) % L, 1) for t in v]
    n = len(v)
    if k > 0:
        return [jnp.where(lane < L - k, r[j], r[(j + 1) % n]) for j in range(n)]
    return [jnp.where(lane >= -k, r[j], r[(j + n - 1) % n]) for j in range(n)]


def mul(a, b):
    return [x * y for x, y in zip(a, b)]


def add(*terms):
    total = terms[0]
    for t in terms[1:]:
        total = [x + y for x, y in zip(total, t)]
    return total


def band(c, shift):
    a = shift(c, -1)
    d = [1.0 - x - y for x, y in zip(c, a)]
    p0 = add(mul(d, d), mul(c, c), mul(a, a))
    p1 = mul(c, add(d, shift(d, 1)))
    p2 = mul(c, shift(c, 1))
    n1, n2 = shift(p1, -1), shift(p2, -2)
    up1 = shift(p1, 1)
    b0 = add(mul(p0, p0), mul(p1, p1), mul(p2, p2), mul(n1, n1), mul(n2, n2))
    b1 = add(mul(p1, add(p0, shift(p0, 1))), mul(p2, up1), mul(n1, shift(p2, -1)))
    b2 = add(mul(p0, p2), mul(p1, up1), mul(p2, shift(p0, 2)))
    b3 = add(mul(p1, shift(p2, 1)), mul(p2, shift(p1, 2)))
    b4 = mul(p2, shift(p2, 2))
    return [shift(b4, -4), shift(b3, -3), shift(b2, -2), shift(b1, -1), b0, b1, b2, b3, b4]


def sweep(w, v, shift, keep=3):
    total = None
    for m in range(2 * M + 1):
        moved = shift(v, m - M)[:keep]
        term = [w(m, j) * t for j, t in enumerate(moved)]
        total = term if total is None else add(total, term)
    return total


def tri(u, d, e):
    eu = e * u
    return d * u + e * pltpu.roll(u, u.shape[0] - 1, 0) + pltpu.roll(eu, 1, 0)


def kernel(
    h_own, h_key, h_sten, h_itp, h_inn, h_wgt, h_c, h_cx, h_cy, o_r, o_q, o_p, o_k,
    own, key, sten, itp, inn, wgt, cyin, s_in, wx, wy,
    keys, vals, metaq, pbuf, sw, sd, sm, rw, rd, rm, rhs, tid, acc,
    tfield, tsend, bfield, bsend, cyfield, cysend, cc, halo, text, bext, cyx,
    ubuf, gbuf, abuf, rbuf, qbuf, dots, red1, red2, onehot, shares_of,
    s_m, s_w, s_d, r_m, r_w, r_d, s_t, r_t, s_b, r_b, s_c, r_c, s_h, r_h, s_1, r_1, s_2, r_2, s_o,
):
    px = lax.axis_index("px")
    py = lax.axis_index("py")

    def ypeer(k):
        return lax.rem(px + k, NPX)

    def opeer(k):
        k = lax.rem(k + lax.rem(px, 2) * (2 * NPY - 2 * k), NPY)
        x = lax.rem(py // 4 + lax.rem(k, 4), 4)
        z = lax.rem(lax.rem(py, 4) + k // 4 + 4 - lax.rem(k, 4), 4)
        return x * 4 + z

    loads = [(h_own, own), (h_key, key), (h_sten, sten), (h_itp, itp), (h_wgt, wgt), (h_inn, inn), (h_cy, cyin)]
    for j in range(2):
        lanes = slice(j * L, (j + 1) * L)
        loads.append((h_c.at[:, :, lanes], cc.at[j, 0:2]))
        loads.append((h_cx.at[:, lanes], cc.at[j, 2]))
    loads = [pltpu.make_async_copy(a, b, s_in.at[n]) for n, (a, b) in enumerate(loads)]
    for load in loads:
        load.start()

    barrier = pltpu.get_barrier_semaphore()

    def greet_px(k, carry):
        pl.semaphore_signal(barrier, inc=1, device_id={"px": ypeer(k)}, device_id_type=MESH)
        return carry

    def greet_py(k, carry):
        pl.semaphore_signal(barrier, inc=1, device_id={"py": opeer(k)}, device_id_type=MESH)
        return carry

    for k in range(1, NPX):
        greet_px(k, 0)
    for k in range(1, NPY):
        greet_py(k, 0)

    for n in range(4):
        loads[n].wait()
    row = iota((L, L), 0)
    col = iota((L, L), 1)
    owner = own[...]
    hit = jnp.concatenate([(owner == d).astype(f32) for d in range(NPY)], axis=0)
    hit16 = hit.astype(bf16)
    upper = (row < col).astype(f32).astype(bf16)
    before = ((row // 8 == col // 8) & (col < row)).astype(f32).astype(bf16)
    inside = dot(hit16, upper)
    count = dot(hit16, jnp.ones((L, L), bf16))
    keys[...] = jnp.where(hit > 0.5, inside + dot(before, count.astype(bf16)), -1.0)

    share = itp[...]
    s_hi, rest = split(share)
    s_hi = s_hi.astype(f32)
    rest = share - s_hi
    s_mid = rest.astype(bf16).astype(f32)
    s_lo = rest - s_mid
    cell = key[...]
    fx = ((cell // NB) * 16 + sten[...]).astype(f32)
    seg = lax.rem(cell, NB).astype(f32)
    zero = jnp.zeros((3, L), f32)
    for bl in range(8):
        pick = [t[bl:bl + 1, :] for t in (s_hi, s_mid, s_lo, fx, seg)] + [zero]
        metaq[:, bl * L:(bl + 1) * L] = jnp.concatenate(pick, axis=0).astype(bf16)

    loads[4].wait()
    loads[5].wait()

    def cut(i, carry):
        rows = pl.ds(pl.multiple_of(i * L, L), L)
        w = wgt[rows, :]
        hi, lo = split(w)
        vals[rows, 0:L] = hi
        vals[rows, L:2 * L] = lo
        hi, lo = split(w * inn[rows, :])
        vals[rows, 2 * L:3 * L] = hi
        vals[rows, 3 * L:4 * L] = lo
        return carry

    lax.fori_loop(0, 8, cut, 0)

    def pack(field, out):
        def one(p, carry):
            out[p, :, 0] = field[:, 2 * p]
            out[p, :, 1] = field[:, 2 * p + 1]
            right = field[:, lax.rem(2 * p + 2, NB)]
            left = field[:, lax.rem(2 * p + NB - 1, NB)]
            out[p, :, 2] = jnp.where(iota(right.shape, right.ndim - 1) < 64, right, left)
            return carry

        lax.fori_loop(0, NPX, one, 0)

    def block(ext, k):
        return ext.at[:, :, :, pl.ds(pl.multiple_of(k * 16, 16), 16), :]

    def turn(send, ext, k, ssem, rsem):
        return pltpu.make_async_remote_copy(
            src_ref=send.at[ypeer(k)], dst_ref=block(ext, px),
            send_sem=ssem.at[k], recv_sem=rsem.at[k],
            device_id={"px": ypeer(k)}, device_id_type=MESH,
        )

    def turned(send, ext, k, ssem, rsem):
        source = lax.rem(px + NPX - k, NPX)
        return pltpu.make_async_remote_copy(
            src_ref=send.at[source], dst_ref=block(ext, source),
            send_sem=ssem.at[k], recv_sem=rsem.at[k],
            device_id={"px": ypeer(k)}, device_id_type=MESH,
        )

    def start_turn(send, ext, ssem, rsem):
        def one(k, carry):
            turn(send, ext, k, ssem, rsem).start()
            return carry

        lax.fori_loop(1, NPX, one, 0)
        ext[:, :, :, pl.ds(pl.multiple_of(px * 16, 16), 16), :] = send[px]

    def end_turn(send, ext, ssem, rsem):
        def one(k, carry):
            turned(send, ext, k, ssem, rsem).wait_recv()
            return carry

        lax.fori_loop(1, NPX, one, 0)


    def edge(side):
        peer = ypeer(1 if side == 1 else NPX - 1)
        return pltpu.make_async_remote_copy(
            src_ref=cc.at[side], dst_ref=halo.at[side],
            send_sem=s_h.at[side], recv_sem=r_h.at[side],
            device_id={"px": peer}, device_id_type=MESH,
        )

    def route(buf, land, k, ssem, rsem):
        return pltpu.make_async_remote_copy(
            src_ref=buf.at[k], dst_ref=land.at[k],
            send_sem=ssem.at[k], recv_sem=rsem.at[k],
            device_id={"py": opeer(k)}, device_id_type=MESH,
        )

    slot = iota((CAP, L), 0).astype(f32)

    def gather(k):
        base = pl.multiple_of(opeer(k) * 8, 8)
        mine = keys[pl.ds(base, 8), :]
        for bl in range(8):
            pbuf[:, bl * L:(bl + 1) * L] = (slot == mine[bl:bl + 1, :]).astype(f32).astype(bf16)
        m = lax.dot_general(metaq[...], pbuf[...], NT, preferred_element_type=f32)
        meta = jnp.concatenate([m[0:1] + m[1:2] + m[2:3], m[4:5] * 32.0 + m[3:4]], axis=0)
        out = dot(pbuf[...], vals[...])
        return meta, out[:, 0:L] + out[:, L:2 * L], out[:, 2 * L:3 * L] + out[:, 3 * L:4 * L]

    def fill_rows(k, carry):
        meta, w, wd = gather(k)
        sm[k] = meta
        sw[k] = w
        sd[k] = wd
        return carry

    lax.fori_loop(1, 6, fill_rows, 0)
    pl.semaphore_wait(barrier, NPX - 1 + NPY - 1)

    def start_rows(k, carry):
        route(sm, rm, k, s_m, r_m).start()
        route(sw, rw, k, s_w, r_w).start()
        return carry

    lax.fori_loop(1, 6, start_rows, 0)

    def send_rows(k, carry):
        meta, w, wd = gather(k)
        sm[k] = meta
        sw[k] = w
        sd[k] = wd
        route(sm, rm, k, s_m, r_m).start()
        route(sw, rw, k, s_w, r_w).start()
        return carry

    lax.fori_loop(6, NPY, send_rows, 0)

    def send_data(k, carry):
        route(sd, rd, k, s_d, r_d).start()
        return carry

    lax.fori_loop(1, NPY, send_data, 0)

    meta, w, wd = gather(0)
    rm[0] = meta
    rw[0] = w
    rd[0] = wd

    for load in loads[6:]:
        load.wait()
    for j in range(2):
        tail = cc[j, 2, L - 8:L, :]
        cc[j, 2, L - 8:L, :] = jnp.where(iota((8, L), 0) < 7, tail, 0.0)
    lanes16 = iota((16, L), 1)
    for b in range(NB):
        tile = cyin[:, b * L:(b + 1) * L]
        if b == NB - 1:
            tile = jnp.where(lanes16 < L - 1, tile, 0.0)
        cyfield[0, b, 0] = tile

    def free_turn(send, ext, ssem, rsem):
        def one(k, carry):
            turn(send, ext, k, ssem, rsem).wait_send()
            return carry

        lax.fori_loop(1, NPX, one, 0)

    pack(cyfield, cysend)

    edge(0).start()
    edge(1).start()
    start_turn(cysend, cyx, s_c, r_c)

    for side in range(2):
        edge(side).wait_recv()
    lanes = iota((L, L), 1)
    for f in range(3):
        cc[2, f] = jnp.where(lanes < 64, halo[0, f], halo[1, f])
    end_turn(cysend, cyx, s_c, r_c)

    CH = 128

    def tiles(count, body, fields=(0, 1)):
        def one(j, carry):
            for f in fields:
                body(j, f)
            return carry

        for j in range(count):
            one(j, 0)

    def chunks(body, fields=(0, 1)):
        def one(i, carry):
            rows = pl.ds(pl.multiple_of(i * CH, CH), CH)
            for f in fields:
                body(f, rows)
            return carry

        lax.fori_loop(0, L // CH, one, 0)

    def bands_x(j, carry):
        for m, w in enumerate(band([cc[j, 2]], xshift)):
            wx[m, j] = w[0]
        return carry

    def bands_y(i, carry):
        rows = pl.ds(pl.multiple_of(i * 16, 16), 16)
        for m, w in enumerate(band([cyx[0, j, 0, rows, :] for j in range(3)], yshift)):
            for j in range(3):
                wy[m, j, rows, :] = w[j]
        return carry

    lax.fori_loop(0, 3, bands_x, 0)
    lax.fori_loop(0, 8, bands_y, 0)

    def sweep_x(v, j):
        return sweep(lambda m, _: wx[m, j], [v], xshift)[0]

    def sweep_y(v, rows, keep=3):
        return sweep(lambda m, j: wy[m, j, rows, :], v, yshift, keep)

    def first_x(j, f):
        ubuf[j, f] = sweep_x(cc[j, f], j)

    def first_y(f, rows):
        v = sweep_y([ubuf[j, f, rows, :] for j in range(3)], rows)
        for j in range(3):
            ubuf[j, f, rows, :] = v[j]

    tiles(3, first_x)
    chunks(first_y)

    pick = jnp.where(iota((8, L), 0) < 3, 1.0, 0.0).astype(bf16)
    target = iota((T, 4 * CAP), 0).astype(f32)

    def group(g, land, buf, ssem, rsem, with_meta, parts):
        for i in range(4):
            k = 4 * g + i

            @pl.when(k > 0)
            def _():
                if with_meta:
                    route(sm, rm, k, s_m, r_m).wait_recv()
                route(buf, land, k, ssem, rsem).wait_recv()

            rows = slice(i * CAP, (i + 1) * CAP)
            if with_meta:
                meta = rm[k]
                s = meta[0:1, :]
                hi = s.astype(bf16).astype(f32)
                mid = (s - hi).astype(bf16).astype(f32)
                three = jnp.concatenate([hi, mid, s - hi - mid, jnp.zeros((5, CAP), f32)], axis=0)
                s = lax.dot_general(three.astype(bf16), pick, TN, preferred_element_type=f32)
                shares_of[k] = s
                tid[0:1, rows] = meta[1:2, :]
            else:
                s = shares_of[k]
            v = land[k]
            va = v * (1.0 - s)
            vs = v * s
            terms = (va * (1.0 - s), vs * s, vs * (1.0 - s)) if parts == 3 else (va, vs)
            for n, term in enumerate(terms):
                hi, lo = split(term)
                rhs[rows, 2 * n * L:(2 * n + 1) * L] = hi
                rhs[rows, (2 * n + 1) * L:(2 * n + 2) * L] = lo
        if with_meta:
            onehot[g] = (target == tid[0:1, :]).astype(f32).astype(bf16)
        width = 2 * parts * L
        part = dot(onehot[g], rhs[:, 0:width])

        @pl.when(g == 0)
        def _():
            acc[:, 0:width] = part

        @pl.when(g > 0)
        def _():
            acc[:, 0:width] += part

    def w_group(g, carry):
        group(g, rw, sw, s_w, r_w, True, 3)
        return carry

    lax.fori_loop(0, 4, w_group, 0)

    def column(n):
        return acc[:, 2 * n * L:(2 * n + 1) * L] + acc[:, (2 * n + 1) * L:(2 * n + 2) * L]

    tfield[0] = (column(0) + pltpu.roll(column(1), 1, 0)).reshape(NB, 2, 16, L)
    tfield[1] = column(2).reshape(NB, 2, 16, L)
    pack(tfield, tsend)
    start_turn(tsend, text, s_t, r_t)

    def d_group(g, carry):
        group(g, rd, sd, s_d, r_d, False, 2)
        return carry

    lax.fori_loop(0, 4, d_group, 0)
    bfield[0] = (column(0) + pltpu.roll(column(1), 1, 0)).reshape(NB, 2, 16, L)

    def b_pack(f, p):
        right = bfield[0, lax.rem(2 * p + 2, NB), f]
        left = bfield[0, lax.rem(2 * p + NB - 1, NB), f]
        return [bfield[0, 2 * p, f], bfield[0, 2 * p + 1, f], jnp.where(lanes16 < 64, right, left)]

    def b_copy(f, k, source):
        return pltpu.make_async_remote_copy(
            src_ref=bsend.at[f, ypeer(k)],
            dst_ref=bext.at[f, :, pl.ds(pl.multiple_of(source * 16, 16), 16), :],
            send_sem=s_b.at[f, k], recv_sem=r_b.at[f, k],
            device_id={"px": ypeer(k)}, device_id_type=MESH,
        )

    for f in range(2):
        def b_send(k, carry, f=f):
            for j, tile in enumerate(b_pack(f, ypeer(k))):
                bsend[f, ypeer(k), j] = tile
            b_copy(f, k, px).start()
            return carry

        for k in (4, 3, 5, 2, 6, 1, 7):
            b_send(k, 0)
    for f in range(2):
        for j, tile in enumerate(b_pack(f, px)):
            bext[f, j, pl.ds(pl.multiple_of(px * 16, 16), 16), :] = tile

    def drain_py(k, carry):
        route(sm, rm, k, s_m, r_m).wait_send()
        route(sw, rw, k, s_w, r_w).wait_send()
        route(sd, rd, k, s_d, r_d).wait_send()
        return carry

    end_turn(tsend, text, s_t, r_t)

    def spread(f, rows, keep=3):
        u = [ubuf[j, f, rows, :] for j in range(3)]
        return u, [tri(u[j], text[0, j, f, rows, :], text[1, j, f, rows, :]) for j in range(3)]

    def mid_chunk(f, rows):
        v = sweep_y(spread(f, rows)[1], rows)
        for j in range(3):
            gbuf[j, f, rows, :] = v[j]

    chunks(mid_chunk)

    def image_start(j, f):
        abuf[j, f] = cc[j, f] + sweep_x(gbuf[j, f], j)

    tiles(3, image_start)

    dots[...] = jnp.zeros_like(dots)

    def add_dot(n, a, b):
        dots[n] += jnp.sum((a * b).reshape(-1, 8, L), axis=0)

    def b_chunk(f, rows):
        v = sweep_y([bext[f, j, rows, :] for j in range(3)], rows)
        for j in range(3):
            gbuf[j, f, rows, :] = v[j]


    def residual_tile(j, f):
        r = sweep_x(gbuf[j, f], j) - abuf[j, f]
        rbuf[j, f] = r

        if j < 2:
            add_dot(0, r, r)

        ubuf[j, f] = sweep_x(r, j)


    def q_chunk(f, rows):
        u = sweep_y([ubuf[j, f, rows, :] for j in range(3)], rows)
        v = [tri(u[j], text[0, j, f, rows, :], text[1, j, f, rows, :]) for j in range(3)]
        for j in range(2):
            add_dot(1, u[j], v[j])
        v = sweep_y(v, rows)
        for j in range(3):
            gbuf[j, f, rows, :] = v[j]


    def q_tile(j, f):
        q = rbuf[j, f] + sweep_x(gbuf[j, f], j)
        qbuf[j, f] = q

        if j < 2:
            add_dot(2, q, q)

        ubuf[j, f] = sweep_x(q, j)


    def p_up(f, rows):
        u = sweep_y([ubuf[j, f, rows, :] for j in range(3)], rows)
        v = [tri(u[j], text[0, j, f, rows, :], text[1, j, f, rows, :]) for j in range(3)]
        for j in range(2):
            add_dot(3, u[j], v[j])
        for j in range(3):
            ubuf[j, f, rows, :] = v[j]

    for f in range(2):
        def b_wait(k, carry, f=f):
            b_copy(f, k, lax.rem(px + NPX - k, NPX)).wait_recv()
            return carry

        lax.fori_loop(1, NPX, b_wait, 0)
        chunks(b_chunk, (f,))
        tiles(3, residual_tile, (f,))
        chunks(q_chunk, (f,))
        tiles(3, q_tile, (f,))
        chunks(p_up, (f,))

    def p_down(f, rows):
        v = sweep_y([ubuf[j, f, rows, :] for j in range(3)], rows, 2)
        for j in range(2):
            gbuf[j, f, rows, :] = v[j]

    def p_tile(j, f):
        abuf[j, f] = qbuf[j, f] + sweep_x(gbuf[j, f], j)

    lines = [jnp.sum(dots[n], axis=0, keepdims=True) for n in range(4)]
    red1[0] = jnp.concatenate(lines + [jnp.zeros((4, L), f32)], axis=0)

    def sum1(k):
        return pltpu.make_async_remote_copy(
            src_ref=red1.at[0], dst_ref=red1.at[k], send_sem=s_1.at[k], recv_sem=r_1.at[k],
            device_id={"px": ypeer(k)}, device_id_type=MESH,
        )

    def sum2(k):
        return pltpu.make_async_remote_copy(
            src_ref=red2.at[0], dst_ref=red2.at[k], send_sem=s_2.at[k], recv_sem=r_2.at[k],
            device_id={"py": opeer(k)}, device_id_type=MESH,
        )

    def put(n, buf, out):
        return [
            pltpu.make_async_copy(buf.at[j], out.at[:, :, j * L:(j + 1) * L], s_o.at[2 * n + j])
            for j in range(2)
        ]

    def merge(count, send, buf):
        for k in range(1, count):
            send(k).wait_recv()
        total = buf[0]
        for k in range(1, count):
            total = total + buf[k]
        return total

    for k in range(1, NPX):
        sum1(k).start()
    outs = put(0, rbuf, o_r) + put(1, qbuf, o_q)
    for copy in outs:
        copy.start()
    chunks(p_down)
    for f in range(2):
        def b_free(k, carry, f=f):
            b_copy(f, k, px).wait_send()
            return carry

        lax.fori_loop(1, NPX, b_free, 0)
    red2[0] = merge(NPX, sum1, red1)
    for k in range(1, NPY):
        sum2(k).start()
    for k in range(1, NPX):
        sum1(k).wait_send()
    tiles(2, p_tile)
    for side in range(2):
        edge(side).wait_send()
    free_turn(cysend, cyx, s_c, r_c)
    free_turn(tsend, text, s_t, r_t)
    lax.fori_loop(1, NPY, drain_py, 0)
    last = put(2, abuf, o_p)
    for copy in last:
        copy.start()
    total = merge(NPY, sum2, red2)
    sums = jnp.sum(total, axis=1, keepdims=True)
    rr, gain, qq, gain2 = [sums[n:n + 1, :] for n in range(4)]
    rq = rr + gain
    qp = qq + gain2
    alpha = rr / rq
    new = alpha * (alpha * qq) - rr
    beta = new / rr
    grow = 1.0 + beta
    alpha2 = new / (grow * grow * rq - 2.0 * alpha * grow * qq + alpha * alpha * qp)
    kr = alpha + alpha2 * grow
    kq = -alpha2 * alpha

    o_k[0:1, :] = jnp.broadcast_to(kr, (1, L))
    o_k[1:2, :] = jnp.broadcast_to(kq, (1, L))
    for copy in outs + last:
        copy.wait()
    for k in range(1, NPY):
        sum2(k).wait_send()


def finish(c, r, q, p, k, control, residual):
    kr = k[0:1, 0:1]
    kq = k[1:2, 0:1]
    for f in range(2):
        control[f] = c[f] + kr * r[f] + kq * q[f]
        residual[f] = r[f] - kr * q[f] - kq * p[f]


def shards(control_start, coef_x, coef_y, innovation, obs_weight, interp, obs_owner, cell_key, stencil):
    dma = pltpu.SemaphoreType.DMA
    vm = pltpu.VMEM
    field = vm((3, 2, L, L), f32)
    scratch = [
        vm((8, L), jnp.int32), vm((8, L), jnp.int32), vm((8, L), jnp.int32), vm((8, L), f32),
        vm((ROWS, L), f32), vm((ROWS, L), f32), vm((16, NB * L), f32), dma((11,)),
        vm((2 * M + 1, 3, L, L), f32), vm((2 * M + 1, 3, L, L), f32),
        vm((L, L), f32), vm((ROWS, 4 * L), bf16), vm((8, ROWS), bf16), vm((CAP, ROWS), bf16),
        vm((NPY, CAP, L), f32), vm((NPY, CAP, L), f32), vm((NPY, 2, CAP), f32),
        vm((NPY, CAP, L), f32), vm((NPY, CAP, L), f32), vm((NPY, 2, CAP), f32),
        vm((4 * CAP, 6 * L), bf16), vm((8, 4 * CAP), f32), vm((T, 6 * L), f32),
        vm((2, NB, 2, 16, L), f32), vm((NPX, 2, 3, 2, 16, L), f32),
        vm((1, NB, 2, 16, L), f32), vm((2, NPX, 3, 16, L), f32),
        vm((1, NB, 1, 16, L), f32), vm((NPX, 1, 3, 1, 16, L), f32),
        vm((3, 3, L, L), f32), vm((2, 3, L, L), f32),
        vm((2, 3, 2, L, L), f32), vm((2, 3, L, L), f32), vm((1, 3, 1, L, L), f32),
        field, field, field, field, field,
        vm((4, 8, L), f32), vm((NPX, 8, L), f32), vm((NPY, 8, L), f32),
        vm((4, T, 4 * CAP), bf16), vm((NPY, CAP, L), f32),
        dma((NPY,)), dma((NPY,)), dma((NPY,)), dma((NPY,)), dma((NPY,)), dma((NPY,)),
        dma((NPX,)), dma((NPX,)), dma((2, NPX)), dma((2, NPX)), dma((NPX,)), dma((NPX,)),
        dma((2,)), dma((2,)), dma((NPX,)), dma((NPX,)), dma((NPY,)), dma((NPY,)), dma((6,)),
    ]
    out = jax.ShapeDtypeStruct((2, L, 2 * L), f32)
    r, q, p, k = pl.pallas_call(
        kernel,
        out_shape=(out, out, out, jax.ShapeDtypeStruct((2, L), f32)),
        in_specs=[pl.BlockSpec(memory_space=pltpu.HBM)] * 9,
        out_specs=(pl.BlockSpec(memory_space=pltpu.HBM),) * 3 + (pl.BlockSpec(memory_space=pltpu.VMEM),),
        scratch_shapes=scratch,
        compiler_params=pltpu.CompilerParams(
            collective_id=0, has_side_effects=True, vmem_limit_bytes=60 * 1024 * 1024
        ),
        name="assimilate",
    )(
        obs_owner.reshape(8, L), cell_key.reshape(8, L), stencil.reshape(8, L), interp.reshape(8, L),
        innovation, obs_weight, control_start.reshape(2, L, 2 * L), coef_x.reshape(L, 2 * L),
        coef_y.reshape(16, NB * L),
    )
    shape = control_start.shape
    control, residual = pl.pallas_call(
        finish, out_shape=(out, out), name="finish",
        in_specs=[pl.BlockSpec(memory_space=pltpu.VMEM)] * 5,
        compiler_params=pltpu.CompilerParams(vmem_limit_bytes=60 * 1024 * 1024),
    )(control_start.reshape(2, L, 2 * L), r, q, p, k)
    return control.reshape(shape), residual.reshape(shape)


def solution(mesh):
    return jax.shard_map(
        shards,
        mesh=mesh,
        in_specs=(
            P(None, "py", None, "px"),
            P("py", None, "px"),
            P("py", "px", None),
            P(("px", "py"), None),
            P(("px", "py"), None),
            P(("px", "py")),
            P(("px", "py"), None),
            P(("px", "py")),
            P(("px", "py")),
        ),
        out_specs=(P(None, "py", None, "px"), P(None, "py", None, "px")),
        check_vma=False,
    )
```
